32 devices in a mesh: slab: 2 (over y), gy: 4 (over z), gx: 4 (over x, core).
Axes of the slice: x: 2, y: 2, z: 4, core: 2. Of those that a mesh axis runs over, the one named last changes fastest.
Arguments:
- volume: float32 [8, 256, 1024], P(None, ('slab', 'gy'), 'gx'), parts along dimension 1, may hold values from -8 to 8
- tissue_mask: int32 [2, 32, 128], P(None, ('slab', 'gy'), 'gx'), parts along dimension 1, may hold values from 0 to 1
- smoothing: float32 [1], replicated, may hold values from 0.7 to 1.4
Outputs:
- filtered: float32 [8, 256, 1024], P(None, ('slab', 'gy'), 'gx'), parts along dimension 1
The draws below stay inside these ranges and needn't reach their ends.
There are 2 independent parts, one for each index of `slab`. The reference program is written for one: setup_inputs(seed, part) draws one part's arguments, and reference() takes and returns one part's arrays. A program takes and returns all parts, laid end to end along the dimension named above; an argument that names none is the same for every part. Nothing has to cross between parts.
All inputs are finite; a program needn't handle non-finite values.
Results may differ from the reference program's by a relative error of at most 0.00002.
Values sent between devices are 32-bit elements; how exact they have to be, the bound alone decides.
A program may use at most 64 MiB of HBM per device.

```python
import jax
import jax.numpy as jnp

Z = 8
ITERS = 2
NY = 128
NX = 1024


def draw_volume(key, part):
    first_key = jax.random.fold_in(key, 11)
    second_key = jax.random.fold_in(key, 12)
    rows_pos = jnp.arange(NY).astype(jnp.float32)
    row_scale = jnp.exp(jnp.log(3.0) * rows_pos / (NY - 1))[None, :, None]
    levels = 1.5 * jax.random.normal(second_key, (Z // 4, NY // 8, NX // 8), jnp.float32)
    spread = jnp.broadcast_to(levels[:, None, :, None, :, None], (Z // 4, 4, NY // 8, 8, NX // 8, 8)).reshape(Z, NY, NX)
    noise = jax.random.normal(first_key, (Z, NY, NX), jnp.float32)
    result = spread + noise * row_scale
    return jnp.clip(result, -8.0, 8.0)


def draw_tissue_mask(key, part):
    mask_key = jax.random.fold_in(key, 21)
    rolls = jax.random.randint(mask_key, (Z // 4, NY // 8, NX // 8), 0, 1000)
    rows_pos = jnp.arange(NY // 8)
    limits = 300 + 600 * rows_pos // max(NY // 8 - 1, 1)
    return (rolls < limits[None, :, None]).astype(jnp.int32)


def setup_inputs(seed: int = 0, part: int = 0) -> dict:
    seeds = jax.random.split(jax.random.key(seed), 4)
    part_splits = jax.random.split(jax.random.fold_in(seeds[3], part), 4)
    return {
        "volume": draw_volume(jax.random.fold_in(jax.random.fold_in(seeds[3], part), 71), part),
        "tissue_mask": draw_tissue_mask(jax.random.fold_in(jax.random.fold_in(seeds[3], part), 71), part),
        "smoothing": jnp.clip(jax.random.uniform(seeds[2], (1,), jnp.float32, 0.7, 1.4), 0.7, 1.4),
    }


OFFSETS = [(a, b, c) for a in (-4, 0, 4) for b in (-8, 0, 8) for c in (-8, 0, 8)]


def expand_mask(tissue_mask):
    blocks_z, blocks_y, blocks_x = tissue_mask.shape
    spread = jnp.broadcast_to(tissue_mask[:, None, :, None, :, None], (blocks_z, 4, blocks_y, 8, blocks_x, 8))
    return spread.reshape(blocks_z * 4, blocks_y * 8, blocks_x * 8).astype(jnp.float32)


def noise_terms(values, tissue):
    residual = values[1:-1] - 0.5 * (values[:-2] + values[2:])
    inner = tissue[1:-1]
    summed = jnp.sum(inner * residual * residual) * (2.0 / 3.0)
    return summed, jnp.sum(inner)


def box_sum(squared, depth, rows, cols):
    first = squared[0:depth] + squared[1:depth + 1] + squared[2:depth + 2]
    second = first[:, 0:rows] + first[:, 1:rows + 1] + first[:, 2:rows + 2]
    return second[:, :, 0:cols] + second[:, :, 1:cols + 1] + second[:, :, 2:cols + 2]


def smooth_once(padded_vals, padded_tiss, values, tissue, inverse_width):
    depth, rows, cols = values.shape
    centre = padded_vals[4:depth + 6, 8:rows + 10, 8:cols + 10]
    numerator = jnp.zeros(values.shape, jnp.float32)
    denominator = jnp.zeros(values.shape, jnp.float32)
    for offset in OFFSETS:
        shift_z, shift_y, shift_x = offset
        moved = padded_vals[4 + shift_z:depth + 6 + shift_z, 8 + shift_y:rows + 10 + shift_y, 8 + shift_x:cols + 10 + shift_x]
        differ = centre - moved
        distance = box_sum(differ * differ, depth, rows, cols)
        other_tiss = padded_tiss[5 + shift_z:5 + shift_z + depth, 9 + shift_y:9 + shift_y + rows, 9 + shift_x:9 + shift_x + cols]
        other_vals = padded_vals[5 + shift_z:5 + shift_z + depth, 9 + shift_y:9 + shift_y + rows, 9 + shift_x:9 + shift_x + cols]
        weight_field = jnp.exp(-distance * inverse_width) * other_tiss
        numerator = numerator + weight_field * other_vals
        denominator = denominator + weight_field
    return tissue * numerator / (denominator + 1.0 - tissue) + (1.0 - tissue) * values


def reference(volume, tissue_mask, smoothing):
    tissue = expand_mask(tissue_mask)
    summed, tissue_count = noise_terms(volume, tissue)
    variance = summed / jnp.maximum(tissue_count, 1.0) + 1e-5
    inverse_width = 1.0 / (54.0 * smoothing[0] * smoothing[0] * variance)
    widths = ((5, 5), (9, 9), (9, 9))
    padded_tiss = jnp.pad(tissue, widths)
    values = volume
    for iteration in range(ITERS):
        padded_vals = jnp.pad(values, widths)
        values = smooth_once(padded_vals, padded_tiss, values, tissue, inverse_width)
    return values
```

```python
import functools

import jax
import jax.numpy as jnp
from jax import lax
from jax.experimental import pallas as pl
from jax.experimental.pallas import tpu as pltpu
from jax.sharding import PartitionSpec as P

MESH = pl.DeviceIdType.MESH
ITERS = 2
SHIFTS = (-9, -8, -7, -1, 0, 1, 7, 8, 9)
DIRS = ((1, 0), (-1, 0), (0, 1), (0, -1), (1, 1), (1, -1), (-1, 1), (-1, -1))


def kernel(
    ny, nx, smooth_ref, vol_ref, mask_ref, out_ref,
    mid, base, shifted, tissue, tissvals, numer, denom, own_tiss, near_tiss, wide_tiss,
    rows_in, row_in, row_out, pack_out, pack_in, corner_in, edge, sums,
    sum_send, sum_recv, halo_send, halo_recv,
):
    depth, rows, cols = vol_ref.shape
    lanes = 128
    tiles = cols // lanes
    blocks_z, blocks_y, blocks_x = mask_ref.shape
    padded = shifted.shape[3]
    peers = ny * nx
    gy, gx = lax.axis_index("gy"), lax.axis_index("gx")
    me = gy * nx + gx

    barrier = pltpu.get_barrier_semaphore()
    for k in range(1, peers):
        flat = lax.rem(me + k, peers)
        pl.semaphore_signal(
            barrier, inc=1, device_id={"gy": flat // nx, "gx": lax.rem(flat, nx)}, device_id_type=MESH
        )

    def exists(dy, dx):
        found = None
        for step, pos, count in ((dy, gy, ny), (dx, gx, nx)):
            if step == 0:
                continue
            here = pos < count - 1 if step > 0 else pos > 0
            found = here if found is None else jnp.logical_and(found, here)
        return found

    def lane_group(shape):
        return lax.broadcasted_iota(jnp.int32, shape, 1) // 16

    def make_packs(src, it):
        group = lane_group((rows, lanes))
        right = jnp.zeros((rows, lanes), jnp.float32)
        left = right
        for z in range(depth):
            high = pltpu.roll(src[z, :, cols - lanes : cols], (16 * z + 16) % lanes, 1)
            right = jnp.where(group == z, high, right)
            low = src[z, :, 0:lanes]
            if z:
                low = pltpu.roll(low, 16 * z, 1)
            left = jnp.where(group == z, low, left)
            row_out[it, 0, z : z + 1] = src[z, rows - 9 : rows - 8, :]
            row_out[it, 1, z : z + 1] = src[z, 8:9, :]
        pack_out[it, 0] = right
        pack_out[it, 1] = left

    def copies(src, it, d):
        dy, dx = DIRS[d]
        pairs = []
        if dx == 0:
            start = rows - 8 if dy > 0 else 0
            pairs.append((src.at[:, start : start + 8, :], rows_in.at[it, d]))
            pairs.append((row_out.at[it, d], row_in.at[it, d]))
        elif dy == 0:
            pairs.append((pack_out.at[it, d - 2], pack_in.at[it, d - 2]))
        else:
            start = rows - 16 if dy > 0 else 0
            pairs.append(
                (pack_out.at[it, 0 if dx > 0 else 1, start : start + 16], corner_in.at[it, d - 4])
            )
        if it == 0:
            pairs.append((own_tiss, near_tiss.at[d]))
        return [
            pltpu.make_async_remote_copy(
                src_ref=a,
                dst_ref=b,
                send_sem=halo_send.at[it, d, j],
                recv_sem=halo_recv.at[it, d, j],
                device_id={"gy": gy + dy, "gx": gx + dx},
                device_id_type=MESH,
            )
            for j, (a, b) in enumerate(pairs)
        ]

    def clear_missing(it):
        for d, (dy, dx) in enumerate(DIRS):

            @pl.when(jnp.logical_not(exists(-dy, -dx)))
            def _():
                if dx == 0:
                    rows_in[it, d] = jnp.zeros(rows_in.shape[2:], jnp.float32)
                    row_in[it, d] = jnp.zeros(row_in.shape[2:], jnp.float32)
                elif dy == 0:
                    pack_in[it, d - 2] = jnp.zeros(pack_in.shape[2:], jnp.float32)
                else:
                    corner_in[it, d - 4] = jnp.zeros(corner_in.shape[2:], jnp.float32)
                if it == 0:
                    near_tiss[d] = jnp.zeros(near_tiss.shape[1:], jnp.float32)

    def start_halo(src, it):
        for d, (dy, dx) in enumerate(DIRS):

            @pl.when(exists(dy, dx))
            def _():
                for copy in copies(src, it, d):
                    copy.start()

    def wait_halo(src, it):
        for d, (dy, dx) in enumerate(DIRS):

            @pl.when(exists(-dy, -dx))
            def _():
                for copy in copies(src, it, d):
                    copy.wait_recv()

    def wait_sent(src, it):
        for d, (dy, dx) in enumerate(DIRS):

            @pl.when(exists(dy, dx))
            def _():
                for copy in copies(src, it, d):
                    copy.wait_send()

    def sum_copy(k):
        flat = lax.rem(me + k, peers)
        return pltpu.make_async_remote_copy(
            src_ref=sums.at[0],
            dst_ref=sums.at[k],
            send_sem=sum_send.at[k],
            recv_sem=sum_recv.at[k],
            device_id={"gy": flat // nx, "gx": lax.rem(flat, nx)},
            device_id_type=MESH,
        )

    def spread_tissue():
        for zb in range(blocks_z):
            first = zb * blocks_y
            wide_tiss[zb, 1 : 1 + blocks_y, lanes : lanes + cols] = own_tiss[first : first + blocks_y]
            wide_tiss[zb, 1 : 1 + blocks_y, 0:lanes] = near_tiss[2, first : first + blocks_y, cols - lanes : cols]
            wide_tiss[zb, 1 : 1 + blocks_y, lanes + cols :] = near_tiss[3, first : first + blocks_y, 0:lanes]
            for row, source, at in ((0, (0, 4, 5), first + blocks_y - 1), (1 + blocks_y, (1, 6, 7), first)):
                mid_d, left_d, right_d = source
                wide_tiss[zb, row : row + 1, lanes : lanes + cols] = near_tiss[mid_d, at : at + 1, :]
                wide_tiss[zb, row : row + 1, 0:lanes] = near_tiss[left_d, at : at + 1, cols - lanes : cols]
                wide_tiss[zb, row : row + 1, lanes + cols :] = near_tiss[right_d, at : at + 1, 0:lanes]
            for ci, c in enumerate((-8, 0, 8)):
                moved = wide_tiss[zb, :, lanes + c : lanes + c + cols]
                for lt in range(tiles):
                    for rb in range(blocks_y + 2):
                        line = moved[rb : rb + 1, lt * lanes : (lt + 1) * lanes]
                        tissue[ci, lt, zb, rb * 8 : rb * 8 + 8] = jnp.broadcast_to(line, (8, lanes))

    def fill_centre(src):
        for z in range(depth):
            base[z, 9 : 9 + rows] = src[z]

    def fill_shifted(it):
        for z in range(depth):
            base[z, 0:1] = row_in[it, 0, z : z + 1]
            base[z, 1:9] = rows_in[it, 0, z]
            base[z, 9 + rows : 17 + rows] = rows_in[it, 1, z]
            base[z, 17 + rows : 18 + rows] = row_in[it, 1, z : z + 1]
        for side, (top, bottom) in enumerate(((0, 2), (1, 3))):
            edge[side, 0:9] = corner_in[it, top, 7:16]
            edge[side, 9 : 9 + rows] = pack_in[it, side]
            edge[side, 9 + rows : 18 + rows] = corner_in[it, bottom, 0:9]
        for z in range(depth):
            left = edge[0]
            if (112 - 16 * z) % lanes:
                left = pltpu.roll(left, (112 - 16 * z) % lanes, 1)
            right = edge[1]
            if z:
                right = pltpu.roll(right, (-16 * z) % lanes, 1)
            whole = jnp.concatenate([left, base[z], right], axis=1)
            for si, d in enumerate(SHIFTS):
                part = whole[:, lanes + d : lanes + d + cols]
                for lt in range(tiles):
                    shifted[si, lt, z] = part[:, lt * lanes : (lt + 1) * lanes]
        for ci in range(3):
            for lt in range(tiles):
                for z in range(depth):
                    vals = shifted[3 * ci + 1, lt, z, 1 : 17 + rows]
                    tissvals[ci, lt, z] = vals * tissue[ci, lt, z // 4]

    def smooth(src, dst, scale):
        numer[...] = jnp.zeros(numer.shape, jnp.float32)
        denom[...] = jnp.zeros(denom.shape, jnp.float32)
        span = rows + 8

        def body(step, carry):
            lt = step // 9
            bi = lax.rem(step // 3, 3)
            ci = lax.rem(step, 3)
            row = pl.multiple_of(bi * 8, 8)

            def squares(zi, a):
                inside, moved = 0 <= zi < depth, 0 <= zi + a < depth
                if not inside and not moved:
                    return None
                total = None
                for k in range(3):
                    if inside:
                        differ = shifted[3 + k, lt, zi, 8 : 8 + span]
                    if moved:
                        other = shifted[3 * ci + k, lt, zi + a, pl.ds(row, span)]
                        differ = differ - other if inside else other
                    part = differ * differ
                    total = part if total is None else total + part
                return total

            for a in (-4, 0, 4):
                low, high = max(0, -a), min(depth, depth - a)
                before, here = squares(low - 1, a), squares(low, a)
                pair = here if before is None else before + here
                for z in range(low, high):
                    after = squares(z + 1, a)
                    cube = pair if after is None else pair + after
                    distance = cube[0:rows] + cube[1 : rows + 1] + cube[2 : rows + 2]
                    weight = jnp.exp(distance * scale)
                    numer[lt, z] += weight * tissvals[ci, lt, z + a, pl.ds(row, rows)]
                    denom[lt, z] += weight * tissue[ci, lt, (z + a) // 4, pl.ds(row, rows)]
                    pair = here if after is None else here + after
                    here = after
            return carry

        lax.fori_loop(0, tiles * 9, body, 0)
        for lt in range(tiles):
            for z in range(depth):
                flag = tissue[1, lt, z // 4, 8 : 8 + rows]
                at = slice(lt * lanes, (lt + 1) * lanes)
                dst[z, :, at] = (
                    flag * numer[lt, z] / (denom[lt, z] + 1.0 - flag) + (1.0 - flag) * src[z, :, at]
                )

    spread = (
        lax.broadcasted_iota(jnp.int32, (blocks_x, cols), 1) // 8
        == lax.broadcasted_iota(jnp.int32, (blocks_x, cols), 0)
    ).astype(jnp.float32)
    for zb in range(blocks_z):
        flags = mask_ref[zb].astype(jnp.float32)
        own_tiss[zb * blocks_y : (zb + 1) * blocks_y] = jnp.dot(
            flags, spread, preferred_element_type=jnp.float32
        )
    total = jnp.zeros((8, cols), jnp.float32)
    count = jnp.zeros((8, cols), jnp.float32)
    for z in range(1, depth - 1):
        residual = vol_ref[z] - 0.5 * (vol_ref[z - 1] + vol_ref[z + 1])
        for yb in range(blocks_y):
            line = (z // 4) * blocks_y + yb
            flag = jnp.broadcast_to(own_tiss[line : line + 1], (8, cols))
            piece = residual[8 * yb : 8 * yb + 8]
            total = total + flag * piece * piece
            count = count + flag
    total = jnp.sum(total, axis=0, keepdims=True)
    count = jnp.sum(count, axis=0, keepdims=True)
    total = functools.reduce(jnp.add, [total[:, i * lanes : (i + 1) * lanes] for i in range(tiles)])
    count = functools.reduce(jnp.add, [count[:, i * lanes : (i + 1) * lanes] for i in range(tiles)])
    sums[0] = jnp.concatenate(
        [jnp.broadcast_to(total, (8, lanes)), jnp.broadcast_to(count, (8, lanes))], axis=0
    )
    make_packs(vol_ref, 0)
    pl.semaphore_wait(barrier, peers - 1)
    start_halo(vol_ref, 0)
    for k in range(1, peers):
        sum_copy(k).start()
    for it in range(ITERS):
        clear_missing(it)
    fill_centre(vol_ref)
    wait_halo(vol_ref, 0)
    spread_tissue()
    fill_shifted(0)
    for k in range(1, peers):
        sum_copy(k).wait_recv()
    everything = sums[0]
    for k in range(1, peers):
        everything = everything + sums[k]
    everything = jnp.sum(everything, axis=1, keepdims=True)
    summed = everything[0:1] * (2.0 / 3.0)
    tissue_count = everything[8:9]
    variance = summed / jnp.maximum(tissue_count, 1.0) + 1e-05
    width = 54.0 * smooth_ref[0] * smooth_ref[0]
    scale = jnp.broadcast_to(-1.0 / (width * variance), (rows, lanes))
    smooth(vol_ref, mid, scale)
    make_packs(mid, 1)
    start_halo(mid, 1)
    fill_centre(mid)
    wait_halo(mid, 1)
    fill_shifted(1)
    smooth(mid, out_ref, scale)
    wait_sent(vol_ref, 0)
    wait_sent(mid, 1)
    for k in range(1, peers):
        sum_copy(k).wait_send()


def on_device(volume, tissue_mask, smoothing):
    ny, nx = lax.axis_size("gy"), lax.axis_size("gx")
    depth, rows, cols = volume.shape
    blocks_z, blocks_y, blocks_x = tissue_mask.shape
    lanes = 128
    tiles = cols // lanes
    padded = -(-(rows + 18) // 8) * 8
    flag_rows = -(-(blocks_y + 2) // 8) * 8
    f32 = jnp.float32
    vmem = pl.BlockSpec(memory_space=pltpu.VMEM)
    return pl.pallas_call(
        functools.partial(kernel, ny, nx),
        out_shape=jax.ShapeDtypeStruct(volume.shape, f32),
        in_specs=[pl.BlockSpec(memory_space=pltpu.SMEM), vmem, vmem],
        out_specs=vmem,
        scratch_shapes=[
            pltpu.VMEM((depth, rows, cols), f32),
            pltpu.VMEM((depth, padded, cols), f32),
            pltpu.VMEM((len(SHIFTS), tiles, depth, padded, lanes), f32),
            pltpu.VMEM((3, tiles, blocks_z, rows + 16, lanes), f32),
            pltpu.VMEM((3, tiles, depth, rows + 16, lanes), f32),
            pltpu.VMEM((tiles, depth, rows, lanes), f32),
            pltpu.VMEM((tiles, depth, rows, lanes), f32),
            pltpu.VMEM((blocks_z * blocks_y, cols), f32),
            pltpu.VMEM((len(DIRS), blocks_z * blocks_y, cols), f32),
            pltpu.VMEM((blocks_z, flag_rows, cols + 2 * lanes), f32),
            pltpu.VMEM((ITERS, 2, depth, 8, cols), f32),
            pltpu.VMEM((ITERS, 2, depth, cols), f32),
            pltpu.VMEM((ITERS, 2, depth, cols), f32),
            pltpu.VMEM((ITERS, 2, rows, lanes), f32),
            pltpu.VMEM((ITERS, 2, rows, lanes), f32),
            pltpu.VMEM((ITERS, 4, 16, lanes), f32),
            pltpu.VMEM((2, padded, lanes), f32),
            pltpu.VMEM((ny * nx, 16, lanes), f32),
            pltpu.SemaphoreType.DMA((ny * nx,)),
            pltpu.SemaphoreType.DMA((ny * nx,)),
            pltpu.SemaphoreType.DMA((ITERS, len(DIRS), 3)),
            pltpu.SemaphoreType.DMA((ITERS, len(DIRS), 3)),
        ],
        compiler_params=pltpu.CompilerParams(collective_id=0, has_side_effects=True),
    )(smoothing, volume, tissue_mask)


def solution(mesh):
    placed = (P(None, ("slab", "gy"), "gx"), P(None, ("slab", "gy"), "gx"), P())
    return jax.shard_map(
        on_device,
        mesh=mesh,
        in_specs=placed,
        out_specs=P(None, ("slab", "gy"), "gx"),
        check_vma=False,
    )
```

```python
import functools

import jax
import jax.numpy as jnp
from jax import lax
from jax.experimental import pallas as pl
from jax.experimental.pallas import tpu as pltpu
from jax.sharding import PartitionSpec as P

MESH = pl.DeviceIdType.MESH
ITERS = 2
LOG2E = 1.4426950408889634
SHIFTS = (-9, -8, -7, -1, 0, 1, 7, 8, 9)
DIRS = ((1, 0), (-1, 0), (0, 1), (0, -1), (1, 1), (1, -1), (-1, 1), (-1, -1))


def kernel(
    ny, nx, smooth_ref, vol_hbm, mask_hbm, out_ref, vol_ref, mask_ref, cubes,
    mid, base, shifted, tissue, tissvals, numer, denom, own_tiss, near_tiss, wide_tiss,
    rows_in, row_in, row_out, pack_out, pack_in, corner_in, edge, sums,
    load_sem, sum_send, sum_recv, halo_send, halo_recv,
):
    depth, rows, cols = vol_ref.shape
    lanes = 128
    tiles = cols // lanes
    blocks_z, blocks_y, blocks_x = mask_ref.shape
    padded = shifted.shape[3]
    peers = ny * nx
    gy, gx = lax.axis_index("gy"), lax.axis_index("gx")
    me = gy * nx + gx

    barrier = pltpu.get_barrier_semaphore()
    for k in range(1, peers):
        flat = lax.rem(me + k, peers)
        pl.semaphore_signal(
            barrier, inc=1, device_id={"gy": flat // nx, "gx": lax.rem(flat, nx)}, device_id_type=MESH
        )

    loads = [
        pltpu.make_async_copy(mask_hbm, mask_ref, load_sem.at[0]),
        pltpu.make_async_copy(vol_hbm, vol_ref, load_sem.at[1]),
    ]
    for load in loads:
        load.start()

    def exists(dy, dx):
        found = None
        for step, pos, count in ((dy, gy, ny), (dx, gx, nx)):
            if step == 0:
                continue
            here = pos < count - 1 if step > 0 else pos > 0
            found = here if found is None else jnp.logical_and(found, here)
        return found

    def lane_group(shape):
        return lax.broadcasted_iota(jnp.int32, shape, 1) // 16

    def make_packs(src, it):
        group = lane_group((rows, lanes))
        right = jnp.zeros((rows, lanes), jnp.float32)
        left = right
        for z in range(depth):
            high = pltpu.roll(src[z, :, cols - lanes : cols], (16 * z + 16) % lanes, 1)
            right = jnp.where(group == z, high, right)
            low = src[z, :, 0:lanes]
            if z:
                low = pltpu.roll(low, 16 * z, 1)
            left = jnp.where(group == z, low, left)
            row_out[it, 0, z : z + 1] = src[z, rows - 9 : rows - 8, :]
            row_out[it, 1, z : z + 1] = src[z, 8:9, :]
        pack_out[it, 0] = right
        pack_out[it, 1] = left

    def copies(src, it, d):
        dy, dx = DIRS[d]
        pairs = []
        if dx == 0:
            start = rows - 8 if dy > 0 else 0
            pairs.append((src.at[:, start : start + 8, :], rows_in.at[it, d]))
            pairs.append((row_out.at[it, d], row_in.at[it, d]))
        elif dy == 0:
            pairs.append((pack_out.at[it, d - 2], pack_in.at[it, d - 2]))
        else:
            start = rows - 16 if dy > 0 else 0
            pairs.append(
                (pack_out.at[it, 0 if dx > 0 else 1, start : start + 16], corner_in.at[it, d - 4])
            )
        if it == 0:
            pairs.append((own_tiss, near_tiss.at[d]))
        return [
            pltpu.make_async_remote_copy(
                src_ref=a,
                dst_ref=b,
                send_sem=halo_send.at[it, d, j],
                recv_sem=halo_recv.at[it, d, j],
                device_id={"gy": gy + dy, "gx": gx + dx},
                device_id_type=MESH,
            )
            for j, (a, b) in enumerate(pairs)
        ]

    def clear_missing(it):
        for d, (dy, dx) in enumerate(DIRS):

            @pl.when(jnp.logical_not(exists(-dy, -dx)))
            def _():
                if dx == 0:
                    rows_in[it, d] = jnp.zeros(rows_in.shape[2:], jnp.float32)
                    row_in[it, d] = jnp.zeros(row_in.shape[2:], jnp.float32)
                elif dy == 0:
                    pack_in[it, d - 2] = jnp.zeros(pack_in.shape[2:], jnp.float32)
                else:
                    corner_in[it, d - 4] = jnp.zeros(corner_in.shape[2:], jnp.float32)
                if it == 0:
                    near_tiss[d] = jnp.zeros(near_tiss.shape[1:], jnp.float32)

    def start_halo(src, it):
        for d, (dy, dx) in enumerate(DIRS):

            @pl.when(exists(dy, dx))
            def _():
                for copy in copies(src, it, d):
                    copy.start()

    def wait_halo(src, it):
        for d, (dy, dx) in enumerate(DIRS):

            @pl.when(exists(-dy, -dx))
            def _():
                for copy in copies(src, it, d):
                    copy.wait_recv()

    def wait_sent(src, it):
        for d, (dy, dx) in enumerate(DIRS):

            @pl.when(exists(dy, dx))
            def _():
                for copy in copies(src, it, d):
                    copy.wait_send()

    def sum_copy(k):
        flat = lax.rem(me + k, peers)
        return pltpu.make_async_remote_copy(
            src_ref=sums.at[0],
            dst_ref=sums.at[k],
            send_sem=sum_send.at[k],
            recv_sem=sum_recv.at[k],
            device_id={"gy": flat // nx, "gx": lax.rem(flat, nx)},
            device_id_type=MESH,
        )

    def spread_tissue():
        for zb in range(blocks_z):
            first = zb * blocks_y
            wide_tiss[zb, 1 : 1 + blocks_y, lanes : lanes + cols] = own_tiss[first : first + blocks_y]
            wide_tiss[zb, 1 : 1 + blocks_y, 0:lanes] = near_tiss[2, first : first + blocks_y, cols - lanes : cols]
            wide_tiss[zb, 1 : 1 + blocks_y, lanes + cols :] = near_tiss[3, first : first + blocks_y, 0:lanes]
            for row, source, at in ((0, (0, 4, 5), first + blocks_y - 1), (1 + blocks_y, (1, 6, 7), first)):
                mid_d, left_d, right_d = source
                wide_tiss[zb, row : row + 1, lanes : lanes + cols] = near_tiss[mid_d, at : at + 1, :]
                wide_tiss[zb, row : row + 1, 0:lanes] = near_tiss[left_d, at : at + 1, cols - lanes : cols]
                wide_tiss[zb, row : row + 1, lanes + cols :] = near_tiss[right_d, at : at + 1, 0:lanes]
            for ci, c in enumerate((-8, 0, 8)):
                moved = wide_tiss[zb, :, lanes + c : lanes + c + cols]
                for lt in range(tiles):
                    for rb in range(blocks_y + 2):
                        line = moved[rb : rb + 1, lt * lanes : (lt + 1) * lanes]
                        tissue[ci, lt, zb, rb * 8 : rb * 8 + 8] = jnp.broadcast_to(line, (8, lanes))

    def fill_centre(src):
        for z in range(depth):
            base[z, 9 : 9 + rows] = src[z]

    def fill_shifted(it):
        for z in range(depth):
            base[z, 0:1] = row_in[it, 0, z : z + 1]
            base[z, 1:9] = rows_in[it, 0, z]
            base[z, 9 + rows : 17 + rows] = rows_in[it, 1, z]
            base[z, 17 + rows : 18 + rows] = row_in[it, 1, z : z + 1]
        for side, (top, bottom) in enumerate(((0, 2), (1, 3))):
            edge[side, 0:9] = corner_in[it, top, 7:16]
            edge[side, 9 : 9 + rows] = pack_in[it, side]
            edge[side, 9 + rows : 18 + rows] = corner_in[it, bottom, 0:9]
        for z in range(depth):
            left = edge[0]
            if (112 - 16 * z) % lanes:
                left = pltpu.roll(left, (112 - 16 * z) % lanes, 1)
            right = edge[1]
            if z:
                right = pltpu.roll(right, (-16 * z) % lanes, 1)
            whole = jnp.concatenate([left, base[z], right], axis=1)
            for si, d in enumerate(SHIFTS):
                part = whole[:, lanes + d : lanes + d + cols]
                for lt in range(tiles):
                    shifted[si, lt, z] = part[:, lt * lanes : (lt + 1) * lanes]
        for ci in range(3):
            for lt in range(tiles):
                for z in range(depth):
                    vals = shifted[3 * ci + 1, lt, z, 1 : 17 + rows]
                    tissvals[ci, lt, z] = vals * tissue[ci, lt, z // 4]

    def smooth(src, dst, scale):
        numer[...] = jnp.zeros(numer.shape, jnp.float32)
        denom[...] = jnp.zeros(denom.shape, jnp.float32)
        span = rows + 8

        def body(step, carry):
            lt = step // 9
            bi = lax.rem(step // 3, 3)
            ci = lax.rem(step, 3)
            row = pl.multiple_of(bi * 8, 8)

            def squares(zi, a):
                inside, moved = 0 <= zi < depth, 0 <= zi + a < depth
                if not inside and not moved:
                    return None
                total = None
                for k in range(3):
                    if inside:
                        differ = shifted[3 + k, lt, zi, 8 : 8 + span]
                    if moved:
                        other = shifted[3 * ci + k, lt, zi + a, pl.ds(row, span)]
                        differ = differ - other if inside else other
                    part = differ * differ
                    total = part if total is None else total + part
                return total

            slot = 0
            for a in (-4, 0, 4):
                low, high = max(0, -a), min(depth, depth - a)
                before, here = squares(low - 1, a), squares(low, a)
                pair = here if before is None else before + here
                for z in range(low, high):
                    after = squares(z + 1, a)
                    cube = pair if after is None else pair + after
                    cubes[slot] = cube
                    distance = cube[0:rows] + cubes[slot, 1 : rows + 1] + cubes[slot, 2 : rows + 2]
                    slot += 1
                    weight = jnp.exp2(distance * scale)
                    numer[lt, z] += weight * tissvals[ci, lt, z + a, pl.ds(row, rows)]
                    denom[lt, z] += weight * tissue[ci, lt, (z + a) // 4, pl.ds(row, rows)]
                    pair = here if after is None else here + after
                    here = after
            return carry

        lax.fori_loop(0, tiles * 9, body, 0)
        for lt in range(tiles):
            for z in range(depth):
                flag = tissue[1, lt, z // 4, 8 : 8 + rows]
                at = slice(lt * lanes, (lt + 1) * lanes)
                dst[z, :, at] = (
                    flag * numer[lt, z] / (denom[lt, z] + 1.0 - flag) + (1.0 - flag) * src[z, :, at]
                )

    loads[0].wait()
    spread = (
        lax.broadcasted_iota(jnp.int32, (blocks_x, cols), 1) // 8
        == lax.broadcasted_iota(jnp.int32, (blocks_x, cols), 0)
    ).astype(jnp.float32)
    for zb in range(blocks_z):
        flags = mask_ref[zb].astype(jnp.float32)
        own_tiss[zb * blocks_y : (zb + 1) * blocks_y] = jnp.dot(
            flags, spread, preferred_element_type=jnp.float32
        )
    loads[1].wait()
    total = jnp.zeros((8, cols), jnp.float32)
    count = jnp.zeros((8, cols), jnp.float32)
    for z in range(1, depth - 1):
        residual = vol_ref[z] - 0.5 * (vol_ref[z - 1] + vol_ref[z + 1])
        for yb in range(blocks_y):
            line = (z // 4) * blocks_y + yb
            flag = jnp.broadcast_to(own_tiss[line : line + 1], (8, cols))
            piece = residual[8 * yb : 8 * yb + 8]
            total = total + flag * piece * piece
            count = count + flag
    total = jnp.sum(total, axis=0, keepdims=True)
    count = jnp.sum(count, axis=0, keepdims=True)
    total = functools.reduce(jnp.add, [total[:, i * lanes : (i + 1) * lanes] for i in range(tiles)])
    count = functools.reduce(jnp.add, [count[:, i * lanes : (i + 1) * lanes] for i in range(tiles)])
    line = lax.broadcasted_iota(jnp.int32, (8, lanes), 0)
    sums[0] = jnp.where(
        line < 4, jnp.broadcast_to(total, (8, lanes)), jnp.broadcast_to(count, (8, lanes))
    )
    make_packs(vol_ref, 0)
    pl.semaphore_wait(barrier, peers - 1)
    for k in range(1, peers):
        sum_copy(k).start()
    start_halo(vol_ref, 0)
    for it in range(ITERS):
        clear_missing(it)
    fill_centre(vol_ref)
    wait_halo(vol_ref, 0)
    spread_tissue()
    fill_shifted(0)
    for k in range(1, peers):
        sum_copy(k).wait_recv()
    everything = sums[0]
    for k in range(1, peers):
        everything = everything + sums[k]
    everything = jnp.sum(everything, axis=1, keepdims=True)
    summed = everything[0:1] * (2.0 / 3.0)
    tissue_count = everything[4:5]
    variance = summed / jnp.maximum(tissue_count, 1.0) + 1e-05
    width = 54.0 * smooth_ref[0] * smooth_ref[0]
    scale = jnp.broadcast_to(-LOG2E / (width * variance), (rows, lanes))
    smooth(vol_ref, mid, scale)
    make_packs(mid, 1)
    start_halo(mid, 1)
    fill_centre(mid)
    wait_halo(mid, 1)
    fill_shifted(1)
    smooth(mid, out_ref, scale)
    wait_sent(vol_ref, 0)
    wait_sent(mid, 1)
    for k in range(1, peers):
        sum_copy(k).wait_send()


def on_device(volume, tissue_mask, smoothing):
    ny, nx = lax.axis_size("gy"), lax.axis_size("gx")
    depth, rows, cols = volume.shape
    blocks_z, blocks_y, blocks_x = tissue_mask.shape
    lanes = 128
    tiles = cols // lanes
    padded = -(-(rows + 18) // 8) * 8
    flag_rows = -(-(blocks_y + 2) // 8) * 8
    f32 = jnp.float32
    vmem = pl.BlockSpec(memory_space=pltpu.VMEM)
    anywhere = pl.BlockSpec(memory_space=pltpu.HBM)
    return pl.pallas_call(
        functools.partial(kernel, ny, nx),
        out_shape=jax.ShapeDtypeStruct(volume.shape, f32),
        in_specs=[pl.BlockSpec(memory_space=pltpu.SMEM), anywhere, anywhere],
        out_specs=vmem,
        scratch_shapes=[
            pltpu.VMEM((depth, rows, cols), f32),
            pltpu.VMEM((blocks_z, blocks_y, blocks_x), jnp.int32),
            pltpu.VMEM((20, rows + 8, lanes), f32),
            pltpu.VMEM((depth, rows, cols), f32),
            pltpu.VMEM((depth, padded, cols), f32),
            pltpu.VMEM((len(SHIFTS), tiles, depth, padded, lanes), f32),
            pltpu.VMEM((3, tiles, blocks_z, rows + 16, lanes), f32),
            pltpu.VMEM((3, tiles, depth, rows + 16, lanes), f32),
            pltpu.VMEM((tiles, depth, rows, lanes), f32),
            pltpu.VMEM((tiles, depth, rows, lanes), f32),
            pltpu.VMEM((blocks_z * blocks_y, cols), f32),
            pltpu.VMEM((len(DIRS), blocks_z * blocks_y, cols), f32),
            pltpu.VMEM((blocks_z, flag_rows, cols + 2 * lanes), f32),
            pltpu.VMEM((ITERS, 2, depth, 8, cols), f32),
            pltpu.VMEM((ITERS, 2, depth, cols), f32),
            pltpu.VMEM((ITERS, 2, depth, cols), f32),
            pltpu.VMEM((ITERS, 2, rows, lanes), f32),
            pltpu.VMEM((ITERS, 2, rows, lanes), f32),
            pltpu.VMEM((ITERS, 4, 16, lanes), f32),
            pltpu.VMEM((2, padded, lanes), f32),
            pltpu.VMEM((ny * nx, 8, lanes), f32),
            pltpu.SemaphoreType.DMA((2,)),
            pltpu.SemaphoreType.DMA((ny * nx,)),
            pltpu.SemaphoreType.DMA((ny * nx,)),
            pltpu.SemaphoreType.DMA((ITERS, len(DIRS), 3)),
            pltpu.SemaphoreType.DMA((ITERS, len(DIRS), 3)),
        ],
        compiler_params=pltpu.CompilerParams(
            collective_id=0, has_side_effects=True, vmem_limit_bytes=16 * 2**20
        ),
    )(smoothing, volume, tissue_mask)


def solution(mesh):
    placed = (P(None, ("slab", "gy"), "gx"), P(None, ("slab", "gy"), "gx"), P())
    return jax.shard_map(
        on_device,
        mesh=mesh,
        in_specs=placed,
        out_specs=P(None, ("slab", "gy"), "gx"),
        check_vma=False,
    )
```

```python
import functools

import jax
import jax.numpy as jnp
from jax import lax
from jax.experimental import pallas as pl
from jax.experimental.pallas import tpu as pltpu
from jax.sharding import PartitionSpec as P

MESH = pl.DeviceIdType.MESH
PHASES = ((0, 2), (0, 1), (1, 2))
LOG2E = 1.4426950408889634
SHIFTS = (-9, -8, -7, -1, 0, 1, 7, 8, 9)
DIRS = ((1, 0), (-1, 0), (0, 1), (0, -1), (1, 1), (1, -1), (-1, 1), (-1, -1))


def kernel(
    ny, nx, smooth_ref, vol_hbm, mask_hbm, out_ref, vol_ref, mask_ref, cubes,
    mid, base, shifted, tissue, tissvals, numer, denom, own_tiss, near_tiss, wide_tiss,
    rows_in, row_in, row_out, pack_out, pack_in, corner_in, edge, sums,
    load_sem, sum_send, sum_recv, halo_send, halo_recv,
):
    depth, rows, cols = vol_ref.shape
    lanes = 128
    tiles = cols // lanes
    blocks_z, blocks_y, blocks_x = mask_ref.shape
    padded = shifted.shape[3]
    peers = ny * nx
    half = depth // 2
    phases = [(low * half, high * half) for low, high in PHASES]
    gy, gx = lax.axis_index("gy"), lax.axis_index("gx")
    me = gy * nx + gx

    barrier = pltpu.get_barrier_semaphore()
    for k in range(1, peers):
        flat = lax.rem(me + k, peers)
        pl.semaphore_signal(
            barrier, inc=1, device_id={"gy": flat // nx, "gx": lax.rem(flat, nx)}, device_id_type=MESH
        )

    loads = [
        pltpu.make_async_copy(mask_hbm, mask_ref, load_sem.at[0]),
        pltpu.make_async_copy(vol_hbm, vol_ref, load_sem.at[1]),
    ]
    for load in loads:
        load.start()

    def exists(dy, dx):
        found = None
        for step, pos, count in ((dy, gy, ny), (dx, gx, nx)):
            if step == 0:
                continue
            here = pos < count - 1 if step > 0 else pos > 0
            found = here if found is None else jnp.logical_and(found, here)
        return found

    def lane_group(shape):
        return lax.broadcasted_iota(jnp.int32, shape, 1) // 16

    def make_packs(src, it):
        group = lane_group((rows, lanes))
        right = jnp.zeros((rows, lanes), jnp.float32)
        left = right
        for z in range(*phases[it]):
            high = pltpu.roll(src[z, :, cols - lanes : cols], (16 * z + 16) % lanes, 1)
            right = jnp.where(group == z, high, right)
            low = src[z, :, 0:lanes]
            if z:
                low = pltpu.roll(low, 16 * z, 1)
            left = jnp.where(group == z, low, left)
            row_out[it, 0, z : z + 1] = src[z, rows - 9 : rows - 8, :]
            row_out[it, 1, z : z + 1] = src[z, 8:9, :]
        pack_out[it, 0] = right
        pack_out[it, 1] = left

    def copies(src, it, d):
        dy, dx = DIRS[d]
        pairs = []
        if dx == 0:
            start = rows - 8 if dy > 0 else 0
            low, high = phases[it]
            pairs.append((src.at[low:high, start : start + 8, :], rows_in.at[it, d, low:high]))
            pairs.append((row_out.at[it, d], row_in.at[it, d]))
        elif dy == 0:
            pairs.append((pack_out.at[it, d - 2], pack_in.at[it, d - 2]))
        else:
            start = rows - 16 if dy > 0 else 0
            pairs.append(
                (pack_out.at[it, 0 if dx > 0 else 1, start : start + 16], corner_in.at[it, d - 4])
            )
        if it == 0:
            pairs.append((own_tiss, near_tiss.at[d]))
        return [
            pltpu.make_async_remote_copy(
                src_ref=a,
                dst_ref=b,
                send_sem=halo_send.at[it, d, j],
                recv_sem=halo_recv.at[it, d, j],
                device_id={"gy": gy + dy, "gx": gx + dx},
                device_id_type=MESH,
            )
            for j, (a, b) in enumerate(pairs)
        ]

    def clear_missing(it):
        for d, (dy, dx) in enumerate(DIRS):

            @pl.when(jnp.logical_not(exists(-dy, -dx)))
            def _():
                if dx == 0:
                    rows_in[it, d] = jnp.zeros(rows_in.shape[2:], jnp.float32)
                    row_in[it, d] = jnp.zeros(row_in.shape[2:], jnp.float32)
                elif dy == 0:
                    pack_in[it, d - 2] = jnp.zeros(pack_in.shape[2:], jnp.float32)
                else:
                    corner_in[it, d - 4] = jnp.zeros(corner_in.shape[2:], jnp.float32)
                if it == 0:
                    near_tiss[d] = jnp.zeros(near_tiss.shape[1:], jnp.float32)

    def start_halo(src, it):
        for d, (dy, dx) in enumerate(DIRS):

            @pl.when(exists(dy, dx))
            def _():
                for copy in copies(src, it, d):
                    copy.start()

    def wait_halo(src, it):
        for d, (dy, dx) in enumerate(DIRS):

            @pl.when(exists(-dy, -dx))
            def _():
                for copy in copies(src, it, d):
                    copy.wait_recv()

    def wait_sent(src, it):
        for d, (dy, dx) in enumerate(DIRS):

            @pl.when(exists(dy, dx))
            def _():
                for copy in copies(src, it, d):
                    copy.wait_send()

    def sum_copy(k):
        flat = lax.rem(me + k, peers)
        return pltpu.make_async_remote_copy(
            src_ref=sums.at[0],
            dst_ref=sums.at[k],
            send_sem=sum_send.at[k],
            recv_sem=sum_recv.at[k],
            device_id={"gy": flat // nx, "gx": lax.rem(flat, nx)},
            device_id_type=MESH,
        )

    def spread_tissue():
        for zb in range(blocks_z):
            first = zb * blocks_y
            wide_tiss[zb, 1 : 1 + blocks_y, lanes : lanes + cols] = own_tiss[first : first + blocks_y]
            wide_tiss[zb, 1 : 1 + blocks_y, 0:lanes] = near_tiss[2, first : first + blocks_y, cols - lanes : cols]
            wide_tiss[zb, 1 : 1 + blocks_y, lanes + cols :] = near_tiss[3, first : first + blocks_y, 0:lanes]
            for row, source, at in ((0, (0, 4, 5), first + blocks_y - 1), (1 + blocks_y, (1, 6, 7), first)):
                mid_d, left_d, right_d = source
                wide_tiss[zb, row : row + 1, lanes : lanes + cols] = near_tiss[mid_d, at : at + 1, :]
                wide_tiss[zb, row : row + 1, 0:lanes] = near_tiss[left_d, at : at + 1, cols - lanes : cols]
                wide_tiss[zb, row : row + 1, lanes + cols :] = near_tiss[right_d, at : at + 1, 0:lanes]
            for ci, c in enumerate((-8, 0, 8)):
                moved = wide_tiss[zb, :, lanes + c : lanes + c + cols]
                for lt in range(tiles):
                    for rb in range(blocks_y + 2):
                        line = moved[rb : rb + 1, lt * lanes : (lt + 1) * lanes]
                        tissue[ci, lt, zb, rb * 8 : rb * 8 + 8] = jnp.broadcast_to(line, (8, lanes))

    def fill_centre(src, it):
        for z in range(*phases[it]):
            base[z, 9 : 9 + rows] = src[z]

    def fill_shifted(it):
        for z in range(*phases[it]):
            base[z, 0:1] = row_in[it, 0, z : z + 1]
            base[z, 1:9] = rows_in[it, 0, z]
            base[z, 9 + rows : 17 + rows] = rows_in[it, 1, z]
            base[z, 17 + rows : 18 + rows] = row_in[it, 1, z : z + 1]
        for side, (top, bottom) in enumerate(((0, 2), (1, 3))):
            edge[side, 0:9] = corner_in[it, top, 7:16]
            edge[side, 9 : 9 + rows] = pack_in[it, side]
            edge[side, 9 + rows : 18 + rows] = corner_in[it, bottom, 0:9]
        for z in range(*phases[it]):
            left = edge[0]
            if (112 - 16 * z) % lanes:
                left = pltpu.roll(left, (112 - 16 * z) % lanes, 1)
            right = edge[1]
            if z:
                right = pltpu.roll(right, (-16 * z) % lanes, 1)
            whole = jnp.concatenate([left, base[z], right], axis=1)
            for si, d in enumerate(SHIFTS):
                part = whole[:, lanes + d : lanes + d + cols]
                for lt in range(tiles):
                    shifted[si, lt, z] = part[:, lt * lanes : (lt + 1) * lanes]
        for ci in range(3):
            for lt in range(tiles):
                for z in range(*phases[it]):
                    vals = shifted[3 * ci + 1, lt, z, 1 : 17 + rows]
                    tissvals[ci, lt, z] = vals * tissue[ci, lt, z // 4]

    def clear_sums():
        numer[...] = jnp.zeros(numer.shape, jnp.float32)
        denom[...] = jnp.zeros(denom.shape, jnp.float32)

    def gather(passes, scale):
        span = rows + 8

        def body(step, carry):
            lt = step // 9
            bi = lax.rem(step // 3, 3)
            ci = lax.rem(step, 3)
            row = pl.multiple_of(bi * 8, 8)

            def squares(zi, a):
                inside, moved = 0 <= zi < depth, 0 <= zi + a < depth
                if not inside and not moved:
                    return None
                total = None
                for k in range(3):
                    if inside:
                        differ = shifted[3 + k, lt, zi, 8 : 8 + span]
                    if moved:
                        other = shifted[3 * ci + k, lt, zi + a, pl.ds(row, span)]
                        differ = differ - other if inside else other
                    part = differ * differ
                    total = part if total is None else total + part
                return total

            slot = 0
            for a, low, high in passes:
                before, here = squares(low - 1, a), squares(low, a)
                pair = here if before is None else before + here
                for z in range(low, high):
                    after = squares(z + 1, a)
                    cube = pair if after is None else pair + after
                    cubes[slot] = cube
                    distance = cube[0:rows] + cubes[slot, 1 : rows + 1] + cubes[slot, 2 : rows + 2]
                    slot += 1
                    weight = jnp.exp2(distance * scale)
                    numer[lt, z] += weight * tissvals[ci, lt, z + a, pl.ds(row, rows)]
                    denom[lt, z] += weight * tissue[ci, lt, (z + a) // 4, pl.ds(row, rows)]
                    pair = here if after is None else here + after
                    here = after
            return carry

        lax.fori_loop(0, tiles * 9, body, 0)

    def finish(src, dst, low, high):
        for lt in range(tiles):
            for z in range(low, high):
                flag = tissue[1, lt, z // 4, 8 : 8 + rows]
                at = slice(lt * lanes, (lt + 1) * lanes)
                dst[z, :, at] = (
                    flag * numer[lt, z] / (denom[lt, z] + 1.0 - flag) + (1.0 - flag) * src[z, :, at]
                )

    loads[0].wait()
    spread = (
        lax.broadcasted_iota(jnp.int32, (blocks_x, cols), 1) // 8
        == lax.broadcasted_iota(jnp.int32, (blocks_x, cols), 0)
    ).astype(jnp.float32)
    for zb in range(blocks_z):
        flags = mask_ref[zb].astype(jnp.float32)
        own_tiss[zb * blocks_y : (zb + 1) * blocks_y] = jnp.dot(
            flags, spread, preferred_element_type=jnp.float32
        )
    loads[1].wait()
    total = jnp.zeros((8, cols), jnp.float32)
    count = jnp.zeros((8, cols), jnp.float32)
    for z in range(1, depth - 1):
        residual = vol_ref[z] - 0.5 * (vol_ref[z - 1] + vol_ref[z + 1])
        for yb in range(blocks_y):
            line = (z // 4) * blocks_y + yb
            flag = jnp.broadcast_to(own_tiss[line : line + 1], (8, cols))
            piece = residual[8 * yb : 8 * yb + 8]
            total = total + flag * piece * piece
            count = count + flag
    total = jnp.sum(total, axis=0, keepdims=True)
    count = jnp.sum(count, axis=0, keepdims=True)
    total = functools.reduce(jnp.add, [total[:, i * lanes : (i + 1) * lanes] for i in range(tiles)])
    count = functools.reduce(jnp.add, [count[:, i * lanes : (i + 1) * lanes] for i in range(tiles)])
    line = lax.broadcasted_iota(jnp.int32, (8, lanes), 0)
    sums[0] = jnp.where(
        line < 4, jnp.broadcast_to(total, (8, lanes)), jnp.broadcast_to(count, (8, lanes))
    )
    make_packs(vol_ref, 0)
    pl.semaphore_wait(barrier, peers - 1)
    for k in range(1, peers):
        sum_copy(k).start()
    start_halo(vol_ref, 0)
    for it in range(len(PHASES)):
        clear_missing(it)
    fill_centre(vol_ref, 0)
    clear_sums()
    wait_halo(vol_ref, 0)
    spread_tissue()
    fill_shifted(0)
    for k in range(1, peers):
        sum_copy(k).wait_recv()
    everything = sums[0]
    for k in range(1, peers):
        everything = everything + sums[k]
    everything = jnp.sum(everything, axis=1, keepdims=True)
    summed = everything[0:1] * (2.0 / 3.0)
    tissue_count = everything[4:5]
    variance = summed / jnp.maximum(tissue_count, 1.0) + 1e-05
    width = 54.0 * smooth_ref[0] * smooth_ref[0]
    scale = jnp.broadcast_to(-LOG2E / (width * variance), (rows, lanes))
    for it, passes in ((1, ((0, 0, half), (4, 0, half))), (2, ((0, half, depth), (-4, half, depth)))):
        gather(passes, scale)
        finish(vol_ref, mid, *phases[it])
        make_packs(mid, it)
        start_halo(mid, it)
    clear_sums()
    fill_centre(mid, 1)
    wait_halo(mid, 1)
    fill_shifted(1)
    gather(((0, 0, half - 1),), scale)
    fill_centre(mid, 2)
    wait_halo(mid, 2)
    fill_shifted(2)
    gather(((0, half - 1, depth), (4, 0, half), (-4, half, depth)), scale)
    finish(mid, out_ref, 0, depth)
    wait_sent(vol_ref, 0)
    wait_sent(mid, 1)
    wait_sent(mid, 2)
    for k in range(1, peers):
        sum_copy(k).wait_send()


def on_device(volume, tissue_mask, smoothing):
    ny, nx = lax.axis_size("gy"), lax.axis_size("gx")
    depth, rows, cols = volume.shape
    blocks_z, blocks_y, blocks_x = tissue_mask.shape
    lanes = 128
    tiles = cols // lanes
    padded = -(-(rows + 18) // 8) * 8
    flag_rows = -(-(blocks_y + 2) // 8) * 8
    f32 = jnp.float32
    vmem = pl.BlockSpec(memory_space=pltpu.VMEM)
    anywhere = pl.BlockSpec(memory_space=pltpu.HBM)
    return pl.pallas_call(
        functools.partial(kernel, ny, nx),
        out_shape=jax.ShapeDtypeStruct(volume.shape, f32),
        in_specs=[pl.BlockSpec(memory_space=pltpu.SMEM), anywhere, anywhere],
        out_specs=vmem,
        scratch_shapes=[
            pltpu.VMEM((depth, rows, cols), f32),
            pltpu.VMEM((blocks_z, blocks_y, blocks_x), jnp.int32),
            pltpu.VMEM((20, rows + 8, lanes), f32),
            pltpu.VMEM((depth, rows, cols), f32),
            pltpu.VMEM((depth, padded, cols), f32),
            pltpu.VMEM((len(SHIFTS), tiles, depth, padded, lanes), f32),
            pltpu.VMEM((3, tiles, blocks_z, rows + 16, lanes), f32),
            pltpu.VMEM((3, tiles, depth, rows + 16, lanes), f32),
            pltpu.VMEM((tiles, depth, rows, lanes), f32),
            pltpu.VMEM((tiles, depth, rows, lanes), f32),
            pltpu.VMEM((blocks_z * blocks_y, cols), f32),
            pltpu.VMEM((len(DIRS), blocks_z * blocks_y, cols), f32),
            pltpu.VMEM((blocks_z, flag_rows, cols + 2 * lanes), f32),
            pltpu.VMEM((len(PHASES), 2, depth, 8, cols), f32),
            pltpu.VMEM((len(PHASES), 2, depth, cols), f32),
            pltpu.VMEM((len(PHASES), 2, depth, cols), f32),
            pltpu.VMEM((len(PHASES), 2, rows, lanes), f32),
            pltpu.VMEM((len(PHASES), 2, rows, lanes), f32),
            pltpu.VMEM((len(PHASES), 4, 16, lanes), f32),
            pltpu.VMEM((2, padded, lanes), f32),
            pltpu.VMEM((ny * nx, 8, lanes), f32),
            pltpu.SemaphoreType.DMA((2,)),
            pltpu.SemaphoreType.DMA((ny * nx,)),
            pltpu.SemaphoreType.DMA((ny * nx,)),
            pltpu.SemaphoreType.DMA((len(PHASES), len(DIRS), 3)),
            pltpu.SemaphoreType.DMA((len(PHASES), len(DIRS), 3)),
        ],
        compiler_params=pltpu.CompilerParams(
            collective_id=0, has_side_effects=True, vmem_limit_bytes=16 * 2**20
        ),
    )(smoothing, volume, tissue_mask)


def solution(mesh):
    placed = (P(None, ("slab", "gy"), "gx"), P(None, ("slab", "gy"), "gx"), P())
    return jax.shard_map(
        on_device,
        mesh=mesh,
        in_specs=placed,
        out_specs=P(None, ("slab", "gy"), "gx"),
        check_vma=False,
    )
```

```python
import functools

import jax
import jax.numpy as jnp
from jax import lax
from jax.experimental import pallas as pl
from jax.experimental.pallas import tpu as pltpu
from jax.sharding import PartitionSpec as P

MESH = pl.DeviceIdType.MESH
PHASES = ((0, 2), (0, 1), (1, 2))
LOG2E = 1.4426950408889634
SHIFTS = (-9, -8, -7, -1, 0, 1, 7, 8, 9)
DIRS = ((1, 0), (-1, 0), (0, 1), (0, -1), (1, 1), (1, -1), (-1, 1), (-1, -1))


def kernel(
    ny, nx, smooth_ref, vol_hbm, mask_hbm, out_ref, vol_ref, mask_ref, cubes,
    mid, base, shifted, tissue, tissvals, numer, denom, own_tiss, near_tiss, wide_tiss,
    rows_in, row_in, row_out, pack_out, pack_in, corner_in, edge, sums,
    load_sem, sum_send, sum_recv, halo_send, halo_recv,
):
    depth, rows, cols = vol_ref.shape
    lanes = 128
    tiles = cols // lanes
    blocks_z, blocks_y, blocks_x = mask_ref.shape
    padded = shifted.shape[3]
    peers = ny * nx
    half = depth // 2
    phases = [(low * half, high * half) for low, high in PHASES]
    gy, gx = lax.axis_index("gy"), lax.axis_index("gx")
    me = gy * nx + gx

    barrier = pltpu.get_barrier_semaphore()
    for k in range(1, peers):
        flat = lax.rem(me + k, peers)
        pl.semaphore_signal(
            barrier, inc=1, device_id={"gy": flat // nx, "gx": lax.rem(flat, nx)}, device_id_type=MESH
        )

    loads = [
        pltpu.make_async_copy(mask_hbm, mask_ref, load_sem.at[0]),
        pltpu.make_async_copy(vol_hbm, vol_ref, load_sem.at[1]),
    ]
    for load in loads:
        load.start()

    def exists(dy, dx):
        found = None
        for step, pos, count in ((dy, gy, ny), (dx, gx, nx)):
            if step == 0:
                continue
            here = pos < count - 1 if step > 0 else pos > 0
            found = here if found is None else jnp.logical_and(found, here)
        return found

    def lane_group(shape):
        return lax.broadcasted_iota(jnp.int32, shape, 1) // 16

    def make_packs(src, it):
        group = lane_group((rows, lanes))
        right = jnp.zeros((rows, lanes), jnp.float32)
        left = right
        for z in range(*phases[it]):
            high = pltpu.roll(src[z, :, cols - lanes : cols], (16 * z + 16) % lanes, 1)
            right = jnp.where(group == z, high, right)
            low = src[z, :, 0:lanes]
            if z:
                low = pltpu.roll(low, 16 * z, 1)
            left = jnp.where(group == z, low, left)
            row_out[it, 0, z : z + 1] = src[z, rows - 9 : rows - 8, :]
            row_out[it, 1, z : z + 1] = src[z, 8:9, :]
        pack_out[it, 0] = right
        pack_out[it, 1] = left

    def copies(src, it, d):
        dy, dx = DIRS[d]
        pairs = []
        if dx == 0:
            start = rows - 8 if dy > 0 else 0
            low, high = phases[it]
            pairs.append((src.at[low:high, start : start + 8, :], rows_in.at[it, d, low:high]))
            pairs.append((row_out.at[it, d], row_in.at[it, d]))
        elif dy == 0:
            pairs.append((pack_out.at[it, d - 2], pack_in.at[it, d - 2]))
        else:
            start = rows - 16 if dy > 0 else 0
            pairs.append(
                (pack_out.at[it, 0 if dx > 0 else 1, start : start + 16], corner_in.at[it, d - 4])
            )
        if it == 0:
            at = {1: slice(cols - lanes, cols), -1: slice(0, lanes), 0: slice(0, cols)}[dx]
            pairs.append((own_tiss.at[:, at], near_tiss.at[d, :, at]))
        return [
            pltpu.make_async_remote_copy(
                src_ref=a,
                dst_ref=b,
                send_sem=halo_send.at[it, d, j],
                recv_sem=halo_recv.at[it, d, j],
                device_id={"gy": gy + dy, "gx": gx + dx},
                device_id_type=MESH,
            )
            for j, (a, b) in enumerate(pairs)
        ]

    def clear_missing(it):
        for d, (dy, dx) in enumerate(DIRS):

            @pl.when(jnp.logical_not(exists(-dy, -dx)))
            def _():
                if dx == 0:
                    rows_in[it, d] = jnp.zeros(rows_in.shape[2:], jnp.float32)
                    row_in[it, d] = jnp.zeros(row_in.shape[2:], jnp.float32)
                elif dy == 0:
                    pack_in[it, d - 2] = jnp.zeros(pack_in.shape[2:], jnp.float32)
                else:
                    corner_in[it, d - 4] = jnp.zeros(corner_in.shape[2:], jnp.float32)
                if it == 0:
                    near_tiss[d] = jnp.zeros(near_tiss.shape[1:], jnp.float32)

    def start_halo(src, it):
        for d, (dy, dx) in enumerate(DIRS):

            @pl.when(exists(dy, dx))
            def _():
                for copy in copies(src, it, d):
                    copy.start()

    def wait_halo(src, it):
        for d, (dy, dx) in enumerate(DIRS):

            @pl.when(exists(-dy, -dx))
            def _():
                for copy in copies(src, it, d):
                    copy.wait_recv()

    def wait_sent(src, it):
        for d, (dy, dx) in enumerate(DIRS):

            @pl.when(exists(dy, dx))
            def _():
                for copy in copies(src, it, d):
                    copy.wait_send()

    def sum_copy(k):
        flat = lax.rem(me + k, peers)
        return pltpu.make_async_remote_copy(
            src_ref=sums.at[0],
            dst_ref=sums.at[k],
            send_sem=sum_send.at[k],
            recv_sem=sum_recv.at[k],
            device_id={"gy": flat // nx, "gx": lax.rem(flat, nx)},
            device_id_type=MESH,
        )

    def spread_tissue():
        for zb in range(blocks_z):
            first = zb * blocks_y
            wide_tiss[zb, 1 : 1 + blocks_y, lanes : lanes + cols] = own_tiss[first : first + blocks_y]
            wide_tiss[zb, 1 : 1 + blocks_y, 0:lanes] = near_tiss[2, first : first + blocks_y, cols - lanes : cols]
            wide_tiss[zb, 1 : 1 + blocks_y, lanes + cols :] = near_tiss[3, first : first + blocks_y, 0:lanes]
            for row, source, at in ((0, (0, 4, 5), first + blocks_y - 1), (1 + blocks_y, (1, 6, 7), first)):
                mid_d, left_d, right_d = source
                wide_tiss[zb, row : row + 1, lanes : lanes + cols] = near_tiss[mid_d, at : at + 1, :]
                wide_tiss[zb, row : row + 1, 0:lanes] = near_tiss[left_d, at : at + 1, cols - lanes : cols]
                wide_tiss[zb, row : row + 1, lanes + cols :] = near_tiss[right_d, at : at + 1, 0:lanes]
            for ci, c in enumerate((-8, 0, 8)):
                moved = wide_tiss[zb, :, lanes + c : lanes + c + cols]
                for lt in range(tiles):
                    for rb in range(blocks_y + 2):
                        line = moved[rb : rb + 1, lt * lanes : (lt + 1) * lanes]
                        tissue[ci, lt, zb, rb * 8 : rb * 8 + 8] = jnp.broadcast_to(line, (8, lanes))

    def fill_centre(src, it):
        for z in range(*phases[it]):
            base[z, 9 : 9 + rows] = src[z]

    def fill_shifted(it):
        for z in range(*phases[it]):
            base[z, 0:1] = row_in[it, 0, z : z + 1]
            base[z, 1:9] = rows_in[it, 0, z]
            base[z, 9 + rows : 17 + rows] = rows_in[it, 1, z]
            base[z, 17 + rows : 18 + rows] = row_in[it, 1, z : z + 1]
        for side, (top, bottom) in enumerate(((0, 2), (1, 3))):
            edge[side, 0:9] = corner_in[it, top, 7:16]
            edge[side, 9 : 9 + rows] = pack_in[it, side]
            edge[side, 9 + rows : 18 + rows] = corner_in[it, bottom, 0:9]
        for z in range(*phases[it]):
            left = edge[0]
            if (112 - 16 * z) % lanes:
                left = pltpu.roll(left, (112 - 16 * z) % lanes, 1)
            right = edge[1]
            if z:
                right = pltpu.roll(right, (-16 * z) % lanes, 1)
            whole = jnp.concatenate([left, base[z], right], axis=1)
            for si, d in enumerate(SHIFTS):
                part = whole[:, lanes + d : lanes + d + cols]
                for lt in range(tiles):
                    shifted[si, lt, z] = part[:, lt * lanes : (lt + 1) * lanes]
        for ci in range(3):
            for lt in range(tiles):
                for z in range(*phases[it]):
                    vals = shifted[3 * ci + 1, lt, z, 1 : 17 + rows]
                    tissvals[ci, lt, z] = vals * tissue[ci, lt, z // 4]

    def clear_sums():
        numer[...] = jnp.zeros(numer.shape, jnp.float32)
        denom[...] = jnp.zeros(denom.shape, jnp.float32)

    def gather(passes, scale):
        span = rows + 8

        def body(step, carry):
            lt = step // 9
            bi = lax.rem(step // 3, 3)
            ci = lax.rem(step, 3)
            row = pl.multiple_of(bi * 8, 8)

            def squares(zi, a):
                inside, moved = 0 <= zi < depth, 0 <= zi + a < depth
                if not inside and not moved:
                    return None
                total = None
                for k in range(3):
                    if inside:
                        differ = shifted[3 + k, lt, zi, 8 : 8 + span]
                    if moved:
                        other = shifted[3 * ci + k, lt, zi + a, pl.ds(row, span)]
                        differ = differ - other if inside else other
                    part = differ * differ
                    total = part if total is None else total + part
                return total

            slot = 0
            for a, low, high in passes:
                before, here = squares(low - 1, a), squares(low, a)
                pair = here if before is None else before + here
                for z in range(low, high):
                    after = squares(z + 1, a)
                    cube = pair if after is None else pair + after
                    cubes[slot] = cube
                    distance = cube[0:rows] + cubes[slot, 1 : rows + 1] + cubes[slot, 2 : rows + 2]
                    slot += 1
                    weight = jnp.exp2(distance * scale)
                    numer[lt, z] += weight * tissvals[ci, lt, z + a, pl.ds(row, rows)]
                    denom[lt, z] += weight * tissue[ci, lt, (z + a) // 4, pl.ds(row, rows)]
                    pair = here if after is None else here + after
                    here = after
            return carry

        lax.fori_loop(0, tiles * 9, body, 0)

    def finish(src, dst, low, high):
        for lt in range(tiles):
            for z in range(low, high):
                flag = tissue[1, lt, z // 4, 8 : 8 + rows]
                at = slice(lt * lanes, (lt + 1) * lanes)
                dst[z, :, at] = (
                    flag * numer[lt, z] / (denom[lt, z] + 1.0 - flag) + (1.0 - flag) * src[z, :, at]
                )

    loads[0].wait()
    spread = (
        lax.broadcasted_iota(jnp.int32, (blocks_x, cols), 1) // 8
        == lax.broadcasted_iota(jnp.int32, (blocks_x, cols), 0)
    ).astype(jnp.float32)
    for zb in range(blocks_z):
        flags = mask_ref[zb].astype(jnp.float32)
        own_tiss[zb * blocks_y : (zb + 1) * blocks_y] = jnp.dot(
            flags, spread, preferred_element_type=jnp.float32
        )
    loads[1].wait()
    total = jnp.zeros((8, cols), jnp.float32)
    count = jnp.zeros((8, cols), jnp.float32)
    for z in range(1, depth - 1):
        residual = vol_ref[z] - 0.5 * (vol_ref[z - 1] + vol_ref[z + 1])
        for yb in range(blocks_y):
            line = (z // 4) * blocks_y + yb
            flag = jnp.broadcast_to(own_tiss[line : line + 1], (8, cols))
            piece = residual[8 * yb : 8 * yb + 8]
            total = total + flag * piece * piece
            count = count + flag
    total = jnp.sum(total, axis=0, keepdims=True)
    count = jnp.sum(count, axis=0, keepdims=True)
    total = functools.reduce(jnp.add, [total[:, i * lanes : (i + 1) * lanes] for i in range(tiles)])
    count = functools.reduce(jnp.add, [count[:, i * lanes : (i + 1) * lanes] for i in range(tiles)])
    lane = lax.broadcasted_iota(jnp.int32, (1, lanes), 1)
    sums[0] = jnp.where(
        lane < lanes // 2,
        jnp.sum(total, axis=1, keepdims=True),
        jnp.sum(count, axis=1, keepdims=True),
    )
    make_packs(vol_ref, 0)
    pl.semaphore_wait(barrier, peers - 1)
    for k in range(1, peers):
        sum_copy(k).start()
    start_halo(vol_ref, 0)
    for it in range(len(PHASES)):
        clear_missing(it)
    fill_centre(vol_ref, 0)
    clear_sums()
    wait_halo(vol_ref, 0)
    spread_tissue()
    fill_shifted(0)
    for k in range(1, peers):
        sum_copy(k).wait_recv()
    everything = sums[0]
    for k in range(1, peers):
        everything = everything + sums[k]
    summed = everything[:, 0:1] * (2.0 / 3.0)
    tissue_count = everything[:, lanes // 2 : lanes // 2 + 1]
    variance = summed / jnp.maximum(tissue_count, 1.0) + 1e-05
    width = 54.0 * smooth_ref[0] * smooth_ref[0]
    scale = jnp.broadcast_to(-LOG2E / (width * variance), (rows, lanes))
    for it, passes in ((1, ((0, 0, half), (4, 0, half))), (2, ((0, half, depth), (-4, half, depth)))):
        gather(passes, scale)
        finish(vol_ref, mid, *phases[it])
        make_packs(mid, it)
        start_halo(mid, it)
    clear_sums()
    fill_centre(mid, 1)
    wait_halo(mid, 1)
    fill_shifted(1)
    gather(((0, 0, half - 1),), scale)
    fill_centre(mid, 2)
    wait_halo(mid, 2)
    fill_shifted(2)
    gather(((0, half - 1, depth), (4, 0, half), (-4, half, depth)), scale)
    finish(mid, out_ref, 0, depth)
    wait_sent(vol_ref, 0)
    wait_sent(mid, 1)
    wait_sent(mid, 2)
    for k in range(1, peers):
        sum_copy(k).wait_send()


def on_device(volume, tissue_mask, smoothing):
    ny, nx = lax.axis_size("gy"), lax.axis_size("gx")
    depth, rows, cols = volume.shape
    blocks_z, blocks_y, blocks_x = tissue_mask.shape
    lanes = 128
    tiles = cols // lanes
    padded = -(-(rows + 18) // 8) * 8
    flag_rows = -(-(blocks_y + 2) // 8) * 8
    f32 = jnp.float32
    vmem = pl.BlockSpec(memory_space=pltpu.VMEM)
    anywhere = pl.BlockSpec(memory_space=pltpu.HBM)
    return pl.pallas_call(
        functools.partial(kernel, ny, nx),
        out_shape=jax.ShapeDtypeStruct(volume.shape, f32),
        in_specs=[pl.BlockSpec(memory_space=pltpu.SMEM), anywhere, anywhere],
        out_specs=vmem,
        scratch_shapes=[
            pltpu.VMEM((depth, rows, cols), f32),
            pltpu.VMEM((blocks_z, blocks_y, blocks_x), jnp.int32),
            pltpu.VMEM((20, rows + 8, lanes), f32),
            pltpu.VMEM((depth, rows, cols), f32),
            pltpu.VMEM((depth, padded, cols), f32),
            pltpu.VMEM((len(SHIFTS), tiles, depth, padded, lanes), f32),
            pltpu.VMEM((3, tiles, blocks_z, rows + 16, lanes), f32),
            pltpu.VMEM((3, tiles, depth, rows + 16, lanes), f32),
            pltpu.VMEM((tiles, depth, rows, lanes), f32),
            pltpu.VMEM((tiles, depth, rows, lanes), f32),
            pltpu.VMEM((blocks_z * blocks_y, cols), f32),
            pltpu.VMEM((len(DIRS), blocks_z * blocks_y, cols), f32),
            pltpu.VMEM((blocks_z, flag_rows, cols + 2 * lanes), f32),
            pltpu.VMEM((len(PHASES), 2, depth, 8, cols), f32),
            pltpu.VMEM((len(PHASES), 2, depth, cols), f32),
            pltpu.VMEM((len(PHASES), 2, depth, cols), f32),
            pltpu.VMEM((len(PHASES), 2, rows, lanes), f32),
            pltpu.VMEM((len(PHASES), 2, rows, lanes), f32),
            pltpu.VMEM((len(PHASES), 4, 16, lanes), f32),
            pltpu.VMEM((2, padded, lanes), f32),
            pltpu.VMEM((ny * nx, 1, lanes), f32),
            pltpu.SemaphoreType.DMA((2,)),
            pltpu.SemaphoreType.DMA((ny * nx,)),
            pltpu.SemaphoreType.DMA((ny * nx,)),
            pltpu.SemaphoreType.DMA((len(PHASES), len(DIRS), 3)),
            pltpu.SemaphoreType.DMA((len(PHASES), len(DIRS), 3)),
        ],
        compiler_params=pltpu.CompilerParams(
            collective_id=0, has_side_effects=True, vmem_limit_bytes=16 * 2**20
        ),
    )(smoothing, volume, tissue_mask)


def solution(mesh):
    placed = (P(None, ("slab", "gy"), "gx"), P(None, ("slab", "gy"), "gx"), P())
    return jax.shard_map(
        on_device,
        mesh=mesh,
        in_specs=placed,
        out_specs=P(None, ("slab", "gy"), "gx"),
        check_vma=False,
    )
```

```python
import functools

import jax
import jax.numpy as jnp
from jax import lax
from jax.experimental import pallas as pl
from jax.experimental.pallas import tpu as pltpu
from jax.sharding import PartitionSpec as P

MESH = pl.DeviceIdType.MESH
PHASES = ((0, 2), (0, 1), (1, 2))
LOG2E = 1.4426950408889634
SHIFTS = (-9, -8, -7, -1, 0, 1, 7, 8, 9)
DIRS = ((1, 0), (-1, 0), (0, 1), (0, -1), (1, 1), (1, -1), (-1, 1), (-1, -1))


def kernel(
    ny, nx, smooth_ref, vol_hbm, mask_hbm, out_ref, vol_ref, mask_ref, cubes,
    mid, base, shifted, tissue, tissvals, numer, denom, own_tiss, near_tiss, wide_tiss,
    rows_in, row_in, row_out, pack_out, pack_in, corner_in, edge, sums,
    load_sem, sum_send, sum_recv, halo_send, halo_recv,
):
    depth, rows, cols = vol_ref.shape
    lanes = 128
    tiles = cols // lanes
    blocks_z, blocks_y, blocks_x = mask_ref.shape
    padded = shifted.shape[3]
    peers = ny * nx
    half = depth // 2
    phases = [(low * half, high * half) for low, high in PHASES]
    gy, gx = lax.axis_index("gy"), lax.axis_index("gx")
    me = gy * nx + gx

    barrier = pltpu.get_barrier_semaphore()
    for k in range(1, peers):
        flat = lax.rem(me + k, peers)
        pl.semaphore_signal(
            barrier, inc=1, device_id={"gy": flat // nx, "gx": lax.rem(flat, nx)}, device_id_type=MESH
        )

    loads = [
        pltpu.make_async_copy(mask_hbm, mask_ref, load_sem.at[0]),
        pltpu.make_async_copy(vol_hbm, vol_ref, load_sem.at[1]),
    ]
    for load in loads:
        load.start()

    def exists(dy, dx):
        found = None
        for step, pos, count in ((dy, gy, ny), (dx, gx, nx)):
            if step == 0:
                continue
            here = pos < count - 1 if step > 0 else pos > 0
            found = here if found is None else jnp.logical_and(found, here)
        return found

    def lane_group(shape):
        return lax.broadcasted_iota(jnp.int32, shape, 1) // 16

    def make_packs(src, it):
        group = lane_group((rows, lanes))
        right = jnp.zeros((rows, lanes), jnp.float32)
        left = right
        for z in range(*phases[it]):
            high = pltpu.roll(src[z, :, cols - lanes : cols], (16 * z + 16) % lanes, 1)
            right = jnp.where(group == z, high, right)
            low = src[z, :, 0:lanes]
            if z:
                low = pltpu.roll(low, 16 * z, 1)
            left = jnp.where(group == z, low, left)
            row_out[it, 0, z : z + 1] = src[z, rows - 9 : rows - 8, :]
            row_out[it, 1, z : z + 1] = src[z, 8:9, :]
        pack_out[it, 0] = right
        pack_out[it, 1] = left

    def copies(src, it, d):
        dy, dx = DIRS[d]
        pairs = []
        if dx == 0:
            start = rows - 8 if dy > 0 else 0
            low, high = phases[it]
            pairs.append((src.at[low:high, start : start + 8, :], rows_in.at[it, d, low:high]))
            pairs.append((row_out.at[it, d], row_in.at[it, d]))
        elif dy == 0:
            pairs.append((pack_out.at[it, d - 2], pack_in.at[it, d - 2]))
        else:
            start = rows - 16 if dy > 0 else 0
            pairs.append(
                (pack_out.at[it, 0 if dx > 0 else 1, start : start + 16], corner_in.at[it, d - 4])
            )
        if it == 0:
            at = {1: slice(cols - lanes, cols), -1: slice(0, lanes), 0: slice(0, cols)}[dx]
            pairs.append((own_tiss.at[:, at], near_tiss.at[d, :, at]))
        return [
            pltpu.make_async_remote_copy(
                src_ref=a,
                dst_ref=b,
                send_sem=halo_send.at[it, d, j],
                recv_sem=halo_recv.at[it, d, j],
                device_id={"gy": gy + dy, "gx": gx + dx},
                device_id_type=MESH,
            )
            for j, (a, b) in enumerate(pairs)
        ]

    def clear_missing(it):
        for d, (dy, dx) in enumerate(DIRS):

            @pl.when(jnp.logical_not(exists(-dy, -dx)))
            def _():
                if dx == 0:
                    rows_in[it, d] = jnp.zeros(rows_in.shape[2:], jnp.float32)
                    row_in[it, d] = jnp.zeros(row_in.shape[2:], jnp.float32)
                elif dy == 0:
                    pack_in[it, d - 2] = jnp.zeros(pack_in.shape[2:], jnp.float32)
                else:
                    corner_in[it, d - 4] = jnp.zeros(corner_in.shape[2:], jnp.float32)
                if it == 0:
                    near_tiss[d] = jnp.zeros(near_tiss.shape[1:], jnp.float32)

    def start_halo(src, it):
        for d, (dy, dx) in enumerate(DIRS):

            @pl.when(exists(dy, dx))
            def _():
                for copy in copies(src, it, d):
                    copy.start()

    def wait_halo(src, it):
        for d, (dy, dx) in enumerate(DIRS):

            @pl.when(exists(-dy, -dx))
            def _():
                for copy in copies(src, it, d):
                    copy.wait_recv()

    def wait_sent(src, it):
        for d, (dy, dx) in enumerate(DIRS):

            @pl.when(exists(dy, dx))
            def _():
                for copy in copies(src, it, d):
                    copy.wait_send()

    def sum_copy(k):
        flat = lax.rem(me + k, peers)
        return pltpu.make_async_remote_copy(
            src_ref=sums.at[0],
            dst_ref=sums.at[k],
            send_sem=sum_send.at[k],
            recv_sem=sum_recv.at[k],
            device_id={"gy": flat // nx, "gx": lax.rem(flat, nx)},
            device_id_type=MESH,
        )

    def spread_tissue():
        for zb in range(blocks_z):
            first = zb * blocks_y
            wide_tiss[zb, 1 : 1 + blocks_y, lanes : lanes + cols] = own_tiss[first : first + blocks_y]
            wide_tiss[zb, 1 : 1 + blocks_y, 0:lanes] = near_tiss[2, first : first + blocks_y, cols - lanes : cols]
            wide_tiss[zb, 1 : 1 + blocks_y, lanes + cols :] = near_tiss[3, first : first + blocks_y, 0:lanes]
            for row, source, at in ((0, (0, 4, 5), first + blocks_y - 1), (1 + blocks_y, (1, 6, 7), first)):
                mid_d, left_d, right_d = source
                wide_tiss[zb, row : row + 1, lanes : lanes + cols] = near_tiss[mid_d, at : at + 1, :]
                wide_tiss[zb, row : row + 1, 0:lanes] = near_tiss[left_d, at : at + 1, cols - lanes : cols]
                wide_tiss[zb, row : row + 1, lanes + cols :] = near_tiss[right_d, at : at + 1, 0:lanes]
            for ci, c in enumerate((-8, 0, 8)):
                moved = wide_tiss[zb, :, lanes + c : lanes + c + cols]
                for lt in range(tiles):
                    for rb in range(blocks_y + 2):
                        line = moved[rb : rb + 1, lt * lanes : (lt + 1) * lanes]
                        tissue[ci, lt, zb, rb * 8 : rb * 8 + 8] = jnp.broadcast_to(line, (8, lanes))

    def fill_centre(src, it):
        for z in range(*phases[it]):
            base[z, 9 : 9 + rows] = src[z]

    def fill_shifted(it):
        for z in range(*phases[it]):
            base[z, 0:1] = row_in[it, 0, z : z + 1]
            base[z, 1:9] = rows_in[it, 0, z]
            base[z, 9 + rows : 17 + rows] = rows_in[it, 1, z]
            base[z, 17 + rows : 18 + rows] = row_in[it, 1, z : z + 1]
        for side, (top, bottom) in enumerate(((0, 2), (1, 3))):
            edge[side, 0:9] = corner_in[it, top, 7:16]
            edge[side, 9 : 9 + rows] = pack_in[it, side]
            edge[side, 9 + rows : 18 + rows] = corner_in[it, bottom, 0:9]
        for z in range(*phases[it]):
            left = edge[0]
            if (112 - 16 * z) % lanes:
                left = pltpu.roll(left, (112 - 16 * z) % lanes, 1)
            right = edge[1]
            if z:
                right = pltpu.roll(right, (-16 * z) % lanes, 1)
            whole = jnp.concatenate([left, base[z], right], axis=1)
            for si, d in enumerate(SHIFTS):
                part = whole[:, lanes + d : lanes + d + cols]
                for lt in range(tiles):
                    shifted[si, lt, z] = part[:, lt * lanes : (lt + 1) * lanes]
        for ci in range(3):
            for lt in range(tiles):
                for z in range(*phases[it]):
                    vals = shifted[3 * ci + 1, lt, z, 1 : 17 + rows]
                    tissvals[ci, lt, z] = vals * tissue[ci, lt, z // 4]

    def clear_sums():
        numer[...] = jnp.zeros(numer.shape, jnp.float32)
        denom[...] = jnp.zeros(denom.shape, jnp.float32)

    def gather(passes, scale):
        span = rows + 8

        def body(step, carry):
            lt = step // 9
            bi = lax.rem(step // 3, 3)
            ci = lax.rem(step, 3)
            row = pl.multiple_of(bi * 8, 8)

            def squares(zi, a):
                inside, moved = 0 <= zi < depth, 0 <= zi + a < depth
                if not inside and not moved:
                    return None
                total = None
                for k in range(3):
                    if inside:
                        differ = shifted[3 + k, lt, zi, 8 : 8 + span]
                    if moved:
                        other = shifted[3 * ci + k, lt, zi + a, pl.ds(row, span)]
                        differ = differ - other if inside else other
                    part = differ * differ
                    total = part if total is None else total + part
                return total

            slot = 0
            for a, low, high in passes:
                before, here = squares(low - 1, a), squares(low, a)
                pair = here if before is None else before + here
                for z in range(low, high):
                    after = squares(z + 1, a)
                    cube = pair if after is None else pair + after
                    cubes[slot] = cube
                    distance = cube[0:rows] + cubes[slot, 1 : rows + 1] + cubes[slot, 2 : rows + 2]
                    slot += 1
                    weight = jnp.exp2(distance * scale)
                    numer[lt, z] += weight * tissvals[ci, lt, z + a, pl.ds(row, rows)]
                    denom[lt, z] += weight * tissue[ci, lt, (z + a) // 4, pl.ds(row, rows)]
                    pair = here if after is None else here + after
                    here = after
            return carry

        lax.fori_loop(0, tiles * 9, body, 0)

    def finish(src, dst, low, high):
        for lt in range(tiles):
            for z in range(low, high):
                flag = tissue[1, lt, z // 4, 8 : 8 + rows]
                at = slice(lt * lanes, (lt + 1) * lanes)
                dst[z, :, at] = (
                    flag * numer[lt, z] / (denom[lt, z] + 1.0 - flag) + (1.0 - flag) * src[z, :, at]
                )

    loads[0].wait()
    spread = (
        lax.broadcasted_iota(jnp.int32, (blocks_x, cols), 1) // 8
        == lax.broadcasted_iota(jnp.int32, (blocks_x, cols), 0)
    ).astype(jnp.float32)
    for zb in range(blocks_z):
        flags = mask_ref[zb].astype(jnp.float32)
        own_tiss[zb * blocks_y : (zb + 1) * blocks_y] = jnp.dot(
            flags, spread, preferred_element_type=jnp.float32
        )
    loads[1].wait()
    total = jnp.zeros((8, cols), jnp.float32)
    count = jnp.zeros((8, cols), jnp.float32)
    for z in range(1, depth - 1):
        residual = vol_ref[z] - 0.5 * (vol_ref[z - 1] + vol_ref[z + 1])
        for yb in range(blocks_y):
            line = (z // 4) * blocks_y + yb
            flag = jnp.broadcast_to(own_tiss[line : line + 1], (8, cols))
            piece = residual[8 * yb : 8 * yb + 8]
            total = total + flag * piece * piece
            count = count + flag
    total = jnp.sum(total, axis=0, keepdims=True)
    count = jnp.sum(count, axis=0, keepdims=True)
    total = functools.reduce(jnp.add, [total[:, i * lanes : (i + 1) * lanes] for i in range(tiles)])
    count = functools.reduce(jnp.add, [count[:, i * lanes : (i + 1) * lanes] for i in range(tiles)])
    lane = lax.broadcasted_iota(jnp.int32, (1, lanes), 1)
    sums[0] = jnp.where(
        lane < lanes // 2,
        jnp.sum(total, axis=1, keepdims=True),
        jnp.sum(count, axis=1, keepdims=True),
    )
    make_packs(vol_ref, 0)
    pl.semaphore_wait(barrier, peers - 1)
    for k in range(1, peers):
        sum_copy(k).start()
    start_halo(vol_ref, 0)
    for it in range(len(PHASES)):
        clear_missing(it)
    fill_centre(vol_ref, 0)
    clear_sums()
    wait_halo(vol_ref, 0)
    spread_tissue()
    fill_shifted(0)
    for k in range(1, peers):
        sum_copy(k).wait_recv()
    everything = sums[0]
    for k in range(1, peers):
        everything = everything + sums[k]
    summed = everything[:, 0:1] * (2.0 / 3.0)
    tissue_count = everything[:, lanes // 2 : lanes // 2 + 1]
    variance = summed / jnp.maximum(tissue_count, 1.0) + 1e-05
    width = 54.0 * smooth_ref[0] * smooth_ref[0]
    scale = jnp.broadcast_to(-LOG2E / (width * variance), (rows, lanes))
    for it, passes in ((1, ((0, 0, half), (4, 0, half))), (2, ((0, half, depth), (-4, half, depth)))):
        gather(passes, scale)
        finish(vol_ref, mid, *phases[it])
        make_packs(mid, it)
        start_halo(mid, it)
    clear_sums()
    fill_centre(mid, 1)
    wait_halo(mid, 1)
    fill_shifted(1)
    gather(((0, 0, half - 1),), scale)
    fill_centre(mid, 2)
    wait_halo(mid, 2)
    fill_shifted(2)
    gather(((0, half - 1, depth), (4, 0, half), (-4, half, depth)), scale)
    finish(mid, out_ref, 0, depth)
    wait_sent(vol_ref, 0)
    wait_sent(mid, 1)
    wait_sent(mid, 2)
    for k in range(1, peers):
        sum_copy(k).wait_send()


def on_device(volume, tissue_mask, smoothing):
    ny, nx = lax.axis_size("gy"), lax.axis_size("gx")
    depth, rows, cols = volume.shape
    blocks_z, blocks_y, blocks_x = tissue_mask.shape
    lanes = 128
    tiles = cols // lanes
    padded = -(-(rows + 18) // 8) * 8
    flag_rows = -(-(blocks_y + 2) // 8) * 8
    f32 = jnp.float32
    vmem = pl.BlockSpec(memory_space=pltpu.VMEM)
    anywhere = pl.BlockSpec(memory_space=pltpu.HBM)
    return pl.pallas_call(
        functools.partial(kernel, ny, nx),
        out_shape=jax.ShapeDtypeStruct(volume.shape, f32),
        in_specs=[pl.BlockSpec(memory_space=pltpu.SMEM), anywhere, anywhere],
        out_specs=vmem,
        scratch_shapes=[
            pltpu.VMEM((depth, rows, cols), f32),
            pltpu.VMEM((blocks_z, blocks_y, blocks_x), jnp.int32),
            pltpu.VMEM((20, rows + 8, lanes), f32),
            pltpu.VMEM((depth, rows, cols), f32),
            pltpu.VMEM((depth, padded, cols), f32),
            pltpu.VMEM((len(SHIFTS), tiles, depth, padded, lanes), f32),
            pltpu.VMEM((3, tiles, blocks_z, rows + 16, lanes), f32),
            pltpu.VMEM((3, tiles, depth, rows + 16, lanes), f32),
            pltpu.VMEM((tiles, depth, rows, lanes), f32),
            pltpu.VMEM((tiles, depth, rows, lanes), f32),
            pltpu.VMEM((blocks_z * blocks_y, cols), f32),
            pltpu.VMEM((len(DIRS), blocks_z * blocks_y, cols), f32),
            pltpu.VMEM((blocks_z, flag_rows, cols + 2 * lanes), f32),
            pltpu.VMEM((len(PHASES), 2, depth, 8, cols), f32),
            pltpu.VMEM((len(PHASES), 2, depth, cols), f32),
            pltpu.VMEM((len(PHASES), 2, depth, cols), f32),
            pltpu.VMEM((len(PHASES), 2, rows, lanes), f32),
            pltpu.VMEM((len(PHASES), 2, rows, lanes), f32),
            pltpu.VMEM((len(PHASES), 4, 16, lanes), f32),
            pltpu.VMEM((2, padded, lanes), f32),
            pltpu.VMEM((ny * nx, 1, lanes), f32),
            pltpu.SemaphoreType.DMA((2,)),
            pltpu.SemaphoreType.DMA((ny * nx,)),
            pltpu.SemaphoreType.DMA((ny * nx,)),
            pltpu.SemaphoreType.DMA((len(PHASES), len(DIRS), 3)),
            pltpu.SemaphoreType.DMA((len(PHASES), len(DIRS), 3)),
        ],
        compiler_params=pltpu.CompilerParams(
            collective_id=0, has_side_effects=True, vmem_limit_bytes=16 * 2**20
        ),
    )(
        smoothing,
        pltpu.with_memory_space_constraint(volume, pltpu.HBM),
        pltpu.with_memory_space_constraint(tissue_mask, pltpu.HBM),
    )


def solution(mesh):
    placed = (P(None, ("slab", "gy"), "gx"), P(None, ("slab", "gy"), "gx"), P())
    return jax.shard_map(
        on_device,
        mesh=mesh,
        in_specs=placed,
        out_specs=P(None, ("slab", "gy"), "gx"),
        check_vma=False,
    )
```

```python
import functools

import jax
import jax.numpy as jnp
from jax import lax
from jax.experimental import pallas as pl
from jax.experimental.pallas import tpu as pltpu
from jax.sharding import PartitionSpec as P

MESH = pl.DeviceIdType.MESH
PHASES = ((0, 2), (0, 1), (1, 2))
LOG2E = 1.4426950408889634
SHIFTS = (-9, -8, -7, -1, 0, 1, 7, 8, 9)
DIRS = ((1, 0), (-1, 0), (0, 1), (0, -1), (1, 1), (1, -1), (-1, 1), (-1, -1))


def kernel(
    ny, nx, smooth_ref, vol_hbm, mask_hbm, out_ref, vol_ref, mask_ref, cubes,
    mid, base, shifted, tissue, tissvals, numer, denom, own_tiss, near_tiss, wide_tiss,
    rows_in, row_in, row_out, pack_out, pack_in, corner_in, edge, sums,
    load_sem, sum_send, sum_recv, halo_send, halo_recv,
):
    depth, rows, cols = vol_ref.shape
    lanes = 128
    tiles = cols // lanes
    blocks_z, blocks_y, blocks_x = mask_ref.shape
    padded = shifted.shape[3]
    peers = ny * nx
    half = depth // 2
    phases = [(low * half, high * half) for low, high in PHASES]
    gy, gx = lax.axis_index("gy"), lax.axis_index("gx")
    me = gy * nx + gx

    barrier = pltpu.get_barrier_semaphore()
    for k in range(1, peers):
        flat = lax.rem(me + k, peers)
        pl.semaphore_signal(
            barrier, inc=1, device_id={"gy": flat // nx, "gx": lax.rem(flat, nx)}, device_id_type=MESH
        )

    loads = [
        pltpu.make_async_copy(mask_hbm, mask_ref, load_sem.at[0]),
        pltpu.make_async_copy(vol_hbm, vol_ref, load_sem.at[1]),
    ]
    for load in loads:
        load.start()

    def exists(dy, dx):
        found = None
        for step, pos, count in ((dy, gy, ny), (dx, gx, nx)):
            if step == 0:
                continue
            here = pos < count - 1 if step > 0 else pos > 0
            found = here if found is None else jnp.logical_and(found, here)
        return found

    def lane_group(shape):
        return lax.broadcasted_iota(jnp.int32, shape, 1) // 16

    def make_packs(src, it):
        group = lane_group((rows, lanes))
        right = jnp.zeros((rows, lanes), jnp.float32)
        left = right
        for z in range(*phases[it]):
            high = pltpu.roll(src[z, :, cols - lanes : cols], (16 * z + 16) % lanes, 1)
            right = jnp.where(group == z, high, right)
            low = src[z, :, 0:lanes]
            if z:
                low = pltpu.roll(low, 16 * z, 1)
            left = jnp.where(group == z, low, left)
            row_out[it, 0, z : z + 1] = src[z, rows - 9 : rows - 8, :]
            row_out[it, 1, z : z + 1] = src[z, 8:9, :]
        pack_out[it, 0] = right
        pack_out[it, 1] = left

    def copies(src, it, d):
        dy, dx = DIRS[d]
        pairs = []
        if dx == 0:
            start = rows - 8 if dy > 0 else 0
            low, high = phases[it]
            pairs.append((src.at[low:high, start : start + 8, :], rows_in.at[it, d, low:high]))
            pairs.append((row_out.at[it, d], row_in.at[it, d]))
        elif dy == 0:
            pairs.append((pack_out.at[it, d - 2], pack_in.at[it, d - 2]))
        else:
            start = rows - 16 if dy > 0 else 0
            pairs.append(
                (pack_out.at[it, 0 if dx > 0 else 1, start : start + 16], corner_in.at[it, d - 4])
            )
        if it == 0:
            at = {1: slice(cols - lanes, cols), -1: slice(0, lanes), 0: slice(0, cols)}[dx]
            pairs.append((own_tiss.at[:, at], near_tiss.at[d, :, at]))
        return [
            pltpu.make_async_remote_copy(
                src_ref=a,
                dst_ref=b,
                send_sem=halo_send.at[it, d, j],
                recv_sem=halo_recv.at[it, d, j],
                device_id={"gy": gy + dy, "gx": gx + dx},
                device_id_type=MESH,
            )
            for j, (a, b) in enumerate(pairs)
        ]

    def clear_missing(it):
        for d, (dy, dx) in enumerate(DIRS):

            @pl.when(jnp.logical_not(exists(-dy, -dx)))
            def _():
                if dx == 0:
                    rows_in[it, d] = jnp.zeros(rows_in.shape[2:], jnp.float32)
                    row_in[it, d] = jnp.zeros(row_in.shape[2:], jnp.float32)
                elif dy == 0:
                    pack_in[it, d - 2] = jnp.zeros(pack_in.shape[2:], jnp.float32)
                else:
                    corner_in[it, d - 4] = jnp.zeros(corner_in.shape[2:], jnp.float32)
                if it == 0:
                    near_tiss[d] = jnp.zeros(near_tiss.shape[1:], jnp.float32)

    def start_halo(src, it):
        for d, (dy, dx) in enumerate(DIRS):

            @pl.when(exists(dy, dx))
            def _():
                for copy in copies(src, it, d):
                    copy.start()

    def wait_halo(src, it):
        for d, (dy, dx) in enumerate(DIRS):

            @pl.when(exists(-dy, -dx))
            def _():
                for copy in copies(src, it, d):
                    copy.wait_recv()

    def wait_sent(src, it):
        for d, (dy, dx) in enumerate(DIRS):

            @pl.when(exists(dy, dx))
            def _():
                for copy in copies(src, it, d):
                    copy.wait_send()

    def sum_copy(k):
        flat = lax.rem(me + k, peers)
        return pltpu.make_async_remote_copy(
            src_ref=sums.at[0],
            dst_ref=sums.at[k],
            send_sem=sum_send.at[k],
            recv_sem=sum_recv.at[k],
            device_id={"gy": flat // nx, "gx": lax.rem(flat, nx)},
            device_id_type=MESH,
        )

    def spread_tissue():
        for zb in range(blocks_z):
            first = zb * blocks_y
            wide_tiss[zb, 1 : 1 + blocks_y, lanes : lanes + cols] = own_tiss[first : first + blocks_y]
            wide_tiss[zb, 1 : 1 + blocks_y, 0:lanes] = near_tiss[2, first : first + blocks_y, cols - lanes : cols]
            wide_tiss[zb, 1 : 1 + blocks_y, lanes + cols :] = near_tiss[3, first : first + blocks_y, 0:lanes]
            for row, source, at in ((0, (0, 4, 5), first + blocks_y - 1), (1 + blocks_y, (1, 6, 7), first)):
                mid_d, left_d, right_d = source
                wide_tiss[zb, row : row + 1, lanes : lanes + cols] = near_tiss[mid_d, at : at + 1, :]
                wide_tiss[zb, row : row + 1, 0:lanes] = near_tiss[left_d, at : at + 1, cols - lanes : cols]
                wide_tiss[zb, row : row + 1, lanes + cols :] = near_tiss[right_d, at : at + 1, 0:lanes]
            for ci, c in enumerate((-8, 0, 8)):
                moved = wide_tiss[zb, :, lanes + c : lanes + c + cols]
                for lt in range(tiles):
                    for rb in range(blocks_y + 2):
                        line = moved[rb : rb + 1, lt * lanes : (lt + 1) * lanes]
                        tissue[ci, lt, zb, rb * 8 : rb * 8 + 8] = jnp.broadcast_to(line, (8, lanes))

    def fill_centre(src, it):
        for z in range(*phases[it]):
            base[z, 9 : 9 + rows] = src[z]

    def fill_shifted(it):
        for z in range(*phases[it]):
            base[z, 0:1] = row_in[it, 0, z : z + 1]
            base[z, 1:9] = rows_in[it, 0, z]
            base[z, 9 + rows : 17 + rows] = rows_in[it, 1, z]
            base[z, 17 + rows : 18 + rows] = row_in[it, 1, z : z + 1]
        for side, (top, bottom) in enumerate(((0, 2), (1, 3))):
            edge[side, 0:9] = corner_in[it, top, 7:16]
            edge[side, 9 : 9 + rows] = pack_in[it, side]
            edge[side, 9 + rows : 18 + rows] = corner_in[it, bottom, 0:9]
        for z in range(*phases[it]):
            left = edge[0]
            if (112 - 16 * z) % lanes:
                left = pltpu.roll(left, (112 - 16 * z) % lanes, 1)
            right = edge[1]
            if z:
                right = pltpu.roll(right, (-16 * z) % lanes, 1)
            whole = jnp.concatenate([left, base[z], right], axis=1)
            for si, d in enumerate(SHIFTS):
                part = whole[:, lanes + d : lanes + d + cols]
                for lt in range(tiles):
                    shifted[si, lt, z] = part[:, lt * lanes : (lt + 1) * lanes]
        for ci in range(3):
            for lt in range(tiles):
                for z in range(*phases[it]):
                    vals = shifted[3 * ci + 1, lt, z, 1 : 17 + rows]
                    tissvals[ci, lt, z] = vals * tissue[ci, lt, z // 4]

    def clear_sums():
        numer[...] = jnp.zeros(numer.shape, jnp.float32)
        denom[...] = jnp.zeros(denom.shape, jnp.float32)

    def gather(passes, scale):
        span = rows + 8

        def body(step, carry):
            lt = step // 3
            bi = lax.rem(step, 3)
            row = pl.multiple_of(bi * 8, 8)

            def squares(zi, a, ci):
                inside, moved = 0 <= zi < depth, 0 <= zi + a < depth
                if not inside and not moved:
                    return None
                total = None
                for k in range(3):
                    if inside:
                        differ = shifted[3 + k, lt, zi, 8 : 8 + span]
                    if moved:
                        other = shifted[3 * ci + k, lt, zi + a, pl.ds(row, span)]
                        differ = differ - other if inside else other
                    part = differ * differ
                    total = part if total is None else total + part
                return total

            slot = 0
            for ci in range(3):
                for a, low, high in passes:
                    before, here = squares(low - 1, a, ci), squares(low, a, ci)
                    pair = here if before is None else before + here
                    for z in range(low, high):
                        after = squares(z + 1, a, ci)
                        cube = pair if after is None else pair + after
                        cubes[slot] = cube
                        distance = cube[0:rows] + cubes[slot, 1 : rows + 1] + cubes[slot, 2 : rows + 2]
                        slot += 1
                        weight = jnp.exp2(distance * scale)
                        numer[lt, z] += weight * tissvals[ci, lt, z + a, pl.ds(row, rows)]
                        denom[lt, z] += weight * tissue[ci, lt, (z + a) // 4, pl.ds(row, rows)]
                        pair = here if after is None else here + after
                        here = after
            return carry

        lax.fori_loop(0, tiles * 3, body, 0)

    def finish(src, dst, low, high):
        for lt in range(tiles):
            for z in range(low, high):
                flag = tissue[1, lt, z // 4, 8 : 8 + rows]
                at = slice(lt * lanes, (lt + 1) * lanes)
                dst[z, :, at] = (
                    flag * numer[lt, z] / (denom[lt, z] + 1.0 - flag) + (1.0 - flag) * src[z, :, at]
                )

    loads[0].wait()
    spread = (
        lax.broadcasted_iota(jnp.int32, (blocks_x, cols), 1) // 8
        == lax.broadcasted_iota(jnp.int32, (blocks_x, cols), 0)
    ).astype(jnp.float32)
    for zb in range(blocks_z):
        flags = mask_ref[zb].astype(jnp.float32)
        own_tiss[zb * blocks_y : (zb + 1) * blocks_y] = jnp.dot(
            flags, spread, preferred_element_type=jnp.float32
        )
    loads[1].wait()
    total = jnp.zeros((8, cols), jnp.float32)
    count = jnp.zeros((8, cols), jnp.float32)
    for z in range(1, depth - 1):
        residual = vol_ref[z] - 0.5 * (vol_ref[z - 1] + vol_ref[z + 1])
        for yb in range(blocks_y):
            line = (z // 4) * blocks_y + yb
            flag = jnp.broadcast_to(own_tiss[line : line + 1], (8, cols))
            piece = residual[8 * yb : 8 * yb + 8]
            total = total + flag * piece * piece
            count = count + flag
    total = jnp.sum(total, axis=0, keepdims=True)
    count = jnp.sum(count, axis=0, keepdims=True)
    total = functools.reduce(jnp.add, [total[:, i * lanes : (i + 1) * lanes] for i in range(tiles)])
    count = functools.reduce(jnp.add, [count[:, i * lanes : (i + 1) * lanes] for i in range(tiles)])
    lane = lax.broadcasted_iota(jnp.int32, (1, lanes), 1)
    sums[0] = jnp.where(
        lane < lanes // 2,
        jnp.sum(total, axis=1, keepdims=True),
        jnp.sum(count, axis=1, keepdims=True),
    )
    make_packs(vol_ref, 0)
    pl.semaphore_wait(barrier, peers - 1)
    for k in range(1, peers):
        sum_copy(k).start()
    start_halo(vol_ref, 0)
    for it in range(len(PHASES)):
        clear_missing(it)
    fill_centre(vol_ref, 0)
    clear_sums()
    wait_halo(vol_ref, 0)
    spread_tissue()
    fill_shifted(0)
    for k in range(1, peers):
        sum_copy(k).wait_recv()
    everything = sums[0]
    for k in range(1, peers):
        everything = everything + sums[k]
    summed = everything[:, 0:1] * (2.0 / 3.0)
    tissue_count = everything[:, lanes // 2 : lanes // 2 + 1]
    variance = summed / jnp.maximum(tissue_count, 1.0) + 1e-05
    width = 54.0 * smooth_ref[0] * smooth_ref[0]
    scale = jnp.broadcast_to(-LOG2E / (width * variance), (rows, lanes))
    for it, passes in ((1, ((0, 0, half), (4, 0, half))), (2, ((0, half, depth), (-4, half, depth)))):
        gather(passes, scale)
        finish(vol_ref, mid, *phases[it])
        make_packs(mid, it)
        start_halo(mid, it)
    clear_sums()
    fill_centre(mid, 1)
    wait_halo(mid, 1)
    fill_shifted(1)
    gather(((0, 0, half - 1),), scale)
    fill_centre(mid, 2)
    wait_halo(mid, 2)
    fill_shifted(2)
    gather(((0, half - 1, depth), (4, 0, half), (-4, half, depth)), scale)
    finish(mid, out_ref, 0, depth)
    wait_sent(vol_ref, 0)
    wait_sent(mid, 1)
    wait_sent(mid, 2)
    for k in range(1, peers):
        sum_copy(k).wait_send()


def on_device(volume, tissue_mask, smoothing):
    ny, nx = lax.axis_size("gy"), lax.axis_size("gx")
    depth, rows, cols = volume.shape
    blocks_z, blocks_y, blocks_x = tissue_mask.shape
    lanes = 128
    tiles = cols // lanes
    padded = -(-(rows + 18) // 8) * 8
    flag_rows = -(-(blocks_y + 2) // 8) * 8
    f32 = jnp.float32
    vmem = pl.BlockSpec(memory_space=pltpu.VMEM)
    anywhere = pl.BlockSpec(memory_space=pltpu.HBM)
    return pl.pallas_call(
        functools.partial(kernel, ny, nx),
        out_shape=jax.ShapeDtypeStruct(volume.shape, f32),
        in_specs=[pl.BlockSpec(memory_space=pltpu.SMEM), anywhere, anywhere],
        out_specs=vmem,
        scratch_shapes=[
            pltpu.VMEM((depth, rows, cols), f32),
            pltpu.VMEM((blocks_z, blocks_y, blocks_x), jnp.int32),
            pltpu.VMEM((60, rows + 8, lanes), f32),
            pltpu.VMEM((depth, rows, cols), f32),
            pltpu.VMEM((depth, padded, cols), f32),
            pltpu.VMEM((len(SHIFTS), tiles, depth, padded, lanes), f32),
            pltpu.VMEM((3, tiles, blocks_z, rows + 16, lanes), f32),
            pltpu.VMEM((3, tiles, depth, rows + 16, lanes), f32),
            pltpu.VMEM((tiles, depth, rows, lanes), f32),
            pltpu.VMEM((tiles, depth, rows, lanes), f32),
            pltpu.VMEM((blocks_z * blocks_y, cols), f32),
            pltpu.VMEM((len(DIRS), blocks_z * blocks_y, cols), f32),
            pltpu.VMEM((blocks_z, flag_rows, cols + 2 * lanes), f32),
            pltpu.VMEM((len(PHASES), 2, depth, 8, cols), f32),
            pltpu.VMEM((len(PHASES), 2, depth, cols), f32),
            pltpu.VMEM((len(PHASES), 2, depth, cols), f32),
            pltpu.VMEM((len(PHASES), 2, rows, lanes), f32),
            pltpu.VMEM((len(PHASES), 2, rows, lanes), f32),
            pltpu.VMEM((len(PHASES), 4, 16, lanes), f32),
            pltpu.VMEM((2, padded, lanes), f32),
            pltpu.VMEM((ny * nx, 1, lanes), f32),
            pltpu.SemaphoreType.DMA((2,)),
            pltpu.SemaphoreType.DMA((ny * nx,)),
            pltpu.SemaphoreType.DMA((ny * nx,)),
            pltpu.SemaphoreType.DMA((len(PHASES), len(DIRS), 3)),
            pltpu.SemaphoreType.DMA((len(PHASES), len(DIRS), 3)),
        ],
        compiler_params=pltpu.CompilerParams(
            collective_id=0, has_side_effects=True, vmem_limit_bytes=16 * 2**20
        ),
    )(
        smoothing,
        pltpu.with_memory_space_constraint(volume, pltpu.HBM),
        pltpu.with_memory_space_constraint(tissue_mask, pltpu.HBM),
    )


def solution(mesh):
    placed = (P(None, ("slab", "gy"), "gx"), P(None, ("slab", "gy"), "gx"), P())
    return jax.shard_map(
        on_device,
        mesh=mesh,
        in_specs=placed,
        out_specs=P(None, ("slab", "gy"), "gx"),
        check_vma=False,
    )
```
